256 devices in a mesh: ctx: 32 (over y, z_lo, core), tp: 8 (over z_hi, x).
Axes of the slice: x: 4, y: 4, z: 8 (z_hi: 2, z_lo: 4; z = z_hi * 4 + z_lo), core: 2. Of those that a mesh axis runs over, the one named last changes fastest.
Arguments:
- query_self: bfloat16 [4096, 8192], P('ctx', 'tp'), may hold values from -120 to 120
- key_self: bfloat16 [4096, 1024], P('ctx', 'tp'), may hold values from -6 to 6
- value_self: bfloat16 [4096, 1024], P('ctx', 'tp'), may hold values from -6 to 6
- grad_self: bfloat16 [4096, 8192], P('ctx', 'tp'), may hold values from -6 to 6
- document_id: int32 [4096], replicated, may hold values from 0 to 15, never falling along the last dimension, each value on 1 to 2176 neighbouring positions
- query_cross: bfloat16 [4096, 8192], P('ctx', 'tp'), may hold values from -120 to 120
- image_keys: bfloat16 [2048, 1024], P('ctx', 'tp'), may hold values from -6 to 6
- image_values: bfloat16 [2048, 1024], P('ctx', 'tp'), may hold values from -6 to 6
- grad_cross: bfloat16 [4096, 8192], P('ctx', 'tp'), may hold values from -6 to 6
- image_block: int32 [4096], P('ctx'), may hold values from 0 to 3, never falling along the last dimension, each value on 1 to 2048 neighbouring positions
- gate: float32 [1], replicated, may hold values from 0.2 to 1.2
- w_key: bfloat16 [8192, 1024], P(None, 'tp'), may hold values from -0.0625 to 0.0625
- w_value: bfloat16 [8192, 1024], P(None, 'tp'), may hold values from -0.0625 to 0.0625
Outputs:
- query_grad: bfloat16 [4096, 8192], P('ctx', 'tp')
- key_grad: bfloat16 [4096, 1024], P('ctx', 'tp')
- value_grad: bfloat16 [4096, 1024], P('ctx', 'tp')
- input_grad: bfloat16 [4096, 8192], P('ctx', 'tp')
- cross_query_grad: bfloat16 [4096, 8192], P('ctx', 'tp')
- image_key_grad: bfloat16 [2048, 1024], P('ctx', 'tp')
- image_value_grad: bfloat16 [2048, 1024], P('ctx', 'tp')
- gate_grad: float32 [1], replicated
The draws below stay inside these ranges and needn't reach their ends.
Inputs may be any that keep to these rules, and one draw needn't show every extreme that they name: document_id never falls along the sequence, every document holds at most 2176 tokens, and one holds exactly that many.
All inputs are finite; a program needn't handle non-finite values.
Results may differ from the reference program's by a relative error of at most 0.013.
Values may be sent and summed in bfloat16 or wider, within the bound.
No kernel may reach another device: no remote copies, remote signals or barrier semaphores. Data moves between devices by JAX's collectives and lax.ppermute only.
A program may use at most 128 MiB of HBM per device.

```python
import math
import jax
import jax.numpy as jnp
import numpy as np
from jax import lax

D = 8192
DH = 128
GROUP = 8
TOK_DEV = 128
NIMG = 4
DOCS = 16
KVH = 8
H = 64
SEQ = 4096
IMG = 2048


def clipped_normal(source, shape):
    return jnp.clip(jax.random.normal(source, shape, jnp.float32), -6.0, 6.0)


def self_keys(key):
    return clipped_normal(jax.random.fold_in(key, 101), (SEQ, KVH * DH))


def image_key_table(key):
    return clipped_normal(jax.random.fold_in(key, 201), (IMG, KVH * DH))


def draw_key_self(key, part):
    return self_keys(key).astype(jnp.bfloat16)


def draw_image_keys(key, part):
    return image_key_table(key).astype(jnp.bfloat16)


def draw_query_self(key, part):
    base = clipped_normal(jax.random.fold_in(key, 102), (SEQ, KVH * GROUP * DH))
    return base.astype(jnp.bfloat16)


def draw_query_cross(key, part):
    base = clipped_normal(jax.random.fold_in(key, 202), (SEQ, KVH * GROUP * DH))
    return base.astype(jnp.bfloat16)


def level_of(key, dims, shards, least, high):
    loudness = 1.0
    for position, parts in shards:
        steps = jax.random.uniform(jax.random.fold_in(jax.random.fold_in(key, 6), position), (parts,), jnp.float32, least / len(shards), high / len(shards))
        loudness = loudness * jnp.repeat(jnp.exp(steps), dims[position] // parts).reshape((-1,) + (1,) * (len(dims) - 1 - position))
    return loudness


def profile(number_of, total, limit, lean):
    portions = [(1 << 20) // math.isqrt(grade ** lean) + 1 for grade in range(2, number_of + 1)]
    spare, holding = total - limit - (number_of - 1), [1] * (number_of - 1)
    while spare > 0:
        candidates = [i for i in range(number_of - 1) if holding[i] < limit]
        pool, left = sum([portions[i] for i in candidates]), spare
        for i in candidates:
            more = min(limit - holding[i], max(1, left * portions[i] // pool), spare)
            holding[i] = holding[i] + more
            spare = spare - more
    return np.array([limit] + holding)


def uneven(stream_key, number_of, total, limit, skew):
    if number_of == 2:
        one = jax.random.randint(stream_key, (), max(1, total - limit), min(limit, total - 1) + 1)
        return jnp.stack([one, total - one])
    tallies = jnp.asarray(profile(number_of, total, limit, skew), jnp.int32)
    twos = (number_of - 1) // 2
    giver, sink = tallies[1:1 + 2 * twos:2], tallies[2:2 + 2 * twos:2]
    room = jnp.minimum(giver - 1, limit - sink)
    passed = jax.random.randint(jax.random.fold_in(stream_key, 1), (twos,), 0, 1 << 20) % (room + 1)
    tallies = tallies.at[1:1 + 2 * twos:2].set(giver - passed).at[2:2 + 2 * twos:2].set(sink + passed)
    return tallies[jax.random.permutation(jax.random.fold_in(stream_key, 2), number_of)]


def scatter_about(stream_key, extent, deviation, limit, cuts=(), held_as=jnp.bfloat16):
    drawn = deviation * jax.random.normal(stream_key, extent, jnp.float32)
    if cuts:
        drawn = drawn * level_of(stream_key, extent, cuts, -0.22, 0.18)
    return jnp.clip(drawn, -limit, limit).astype(held_as)


def setup_inputs(seed: int = 0) -> dict:
    arg_keys = jax.random.split(jax.random.key(seed), 14)
    return {
        "query_self": draw_query_self(jax.random.fold_in(arg_keys[13], 71), 0),
        "key_self": draw_key_self(jax.random.fold_in(arg_keys[13], 71), 0),
        "value_self": scatter_about(arg_keys[2], (SEQ, KVH * DH), 1.0, 6.0, ((0, 32), (1, 8))),
        "grad_self": scatter_about(arg_keys[3], (SEQ, H * DH), 1.0, 6.0, ((0, 32), (1, 8))),
        "document_id": jnp.searchsorted(jnp.cumsum(uneven(arg_keys[4], DOCS, SEQ, SEQ // 2 + TOK_DEV, 0)), jnp.arange(SEQ), side="right").astype(jnp.int32),
        "query_cross": draw_query_cross(jax.random.fold_in(arg_keys[13], 71), 0),
        "image_keys": draw_image_keys(jax.random.fold_in(arg_keys[13], 71), 0),
        "image_values": scatter_about(arg_keys[7], (IMG, KVH * DH), 1.0, 6.0, ((0, 32), (1, 8))),
        "grad_cross": scatter_about(arg_keys[8], (SEQ, H * DH), 1.0, 6.0, ((0, 32), (1, 8))),
        "image_block": jnp.searchsorted(jnp.cumsum(uneven(arg_keys[9], NIMG, SEQ, SEQ // 2, 0)), jnp.arange(SEQ), side="right").astype(jnp.int32),
        "gate": jnp.clip(jax.random.uniform(arg_keys[10], (1,), jnp.float32, 0.2, 1.2), 0.2, 1.2),
        "w_key": scatter_about(arg_keys[11], (D, KVH * DH), D ** -0.5, 0.0625, ((1, 8),)),
        "w_value": scatter_about(arg_keys[12], (D, KVH * DH), D ** -0.5, 0.0625, ((1, 8),)),
    }


NEG_FILL = -1.0e30


def round_half(values):
    return lax.optimization_barrier(values.astype(jnp.bfloat16)).astype(jnp.float32)


def self_attention(query_self, key_self, value_self, grad_self, document_id):
    score_scale = DH ** -0.5
    queries = query_self.astype(jnp.float32).reshape(SEQ, KVH, GROUP, DH).transpose(1, 0, 2, 3)
    cotangent = grad_self.astype(jnp.float32).reshape(SEQ, KVH, GROUP, DH).transpose(1, 0, 2, 3)
    key_heads = key_self.astype(jnp.float32).reshape(SEQ, KVH, DH).transpose(1, 0, 2)
    value_heads = value_self.astype(jnp.float32).reshape(SEQ, KVH, DH).transpose(1, 0, 2)
    row_block = min(SEQ, 512)
    block_count = SEQ // row_block
    positions = jnp.arange(SEQ, dtype=jnp.int32)

    def per_head(operands):
        query_head, grad_head, key_head, value_head = operands

        def one_block(state, block_index):
            row_start = (block_index * row_block).astype(jnp.int32)
            query_rows = lax.dynamic_slice_in_dim(query_head, row_start, row_block, 0)
            grad_rows = lax.dynamic_slice_in_dim(grad_head, row_start, row_block, 0)
            query_pos = row_start + jnp.arange(row_block, dtype=jnp.int32)
            query_doc = lax.dynamic_slice_in_dim(document_id, row_start, row_block, 0)
            allowed = ((positions[None, :] <= query_pos[:, None]) & (document_id[None, :] == query_doc[:, None]))[None]
            scores = jnp.where(allowed, jnp.einsum("qhd,kd->hqk", query_rows, key_head) * score_scale, NEG_FILL)
            dprob = jnp.einsum("qhd,kd->hqk", grad_rows, value_head)
            row_peak = jnp.max(scores, axis=-1)
            weights = jnp.where(allowed, jnp.exp(scores - row_peak[..., None]), 0.0)
            row_total = jnp.sum(weights, axis=-1)
            log_sum = row_peak + jnp.log(row_total)
            row_delta = jnp.sum(weights * dprob, axis=-1) / row_total
            prob = jnp.where(allowed, jnp.exp(scores - log_sum[..., None]), 0.0)
            prob_half = round_half(prob)
            dscore = round_half(prob * (dprob - row_delta[..., None]))
            query_part = jnp.einsum("hqk,kd->qhd", dscore, key_head)
            key_acc = state[0] + jnp.einsum("hqk,qhd->kd", dscore, query_rows)
            value_acc = state[1] + jnp.einsum("hqk,qhd->kd", prob_half, grad_rows)
            return (key_acc, value_acc), query_part

        zero_rows = jnp.zeros((SEQ, DH), jnp.float32)
        (key_acc, value_acc), query_parts = lax.scan(one_block, (zero_rows, zero_rows), jnp.arange(block_count, dtype=jnp.int32))
        return query_parts.reshape(SEQ, GROUP, DH), key_acc, value_acc

    query_acc, key_acc, value_acc = lax.map(per_head, (queries, cotangent, key_heads, value_heads))
    query_grad = (query_acc.transpose(1, 0, 2, 3).reshape(SEQ, KVH * GROUP * DH) * score_scale).astype(jnp.bfloat16)
    key_grad = (key_acc.transpose(1, 0, 2).reshape(SEQ, KVH * DH) * score_scale).astype(jnp.bfloat16)
    value_grad = value_acc.transpose(1, 0, 2).reshape(SEQ, KVH * DH).astype(jnp.bfloat16)
    return query_grad, key_grad, value_grad


def cross_attention(query_cross, image_keys, image_values, grad_cross, image_block, tanh_gate):
    score_scale = DH ** -0.5
    queries = query_cross.astype(jnp.float32).reshape(SEQ, KVH, GROUP, DH).transpose(1, 0, 2, 3)
    cotangent = grad_cross.astype(jnp.float32).reshape(SEQ, KVH, GROUP, DH).transpose(1, 0, 2, 3)
    key_heads = image_keys.astype(jnp.float32).reshape(IMG, KVH, DH).transpose(1, 0, 2)
    value_heads = image_values.astype(jnp.float32).reshape(IMG, KVH, DH).transpose(1, 0, 2)
    image_of_key = jnp.arange(IMG, dtype=jnp.int32) // (IMG // NIMG)
    row_block = min(SEQ, 512)
    block_count = SEQ // row_block

    def per_head(operands):
        query_head, grad_head, key_head, value_head = operands

        def one_block(state, block_index):
            row_start = (block_index * row_block).astype(jnp.int32)
            query_rows = lax.dynamic_slice_in_dim(query_head, row_start, row_block, 0)
            grad_rows = lax.dynamic_slice_in_dim(grad_head, row_start, row_block, 0)
            block_rows = lax.dynamic_slice_in_dim(image_block, row_start, row_block, 0)
            allowed = (image_of_key[None, :] <= block_rows[:, None])[None]
            scores = jnp.where(allowed, jnp.einsum("qhd,kd->hqk", query_rows, key_head) * score_scale, NEG_FILL)
            row_peak = jnp.max(scores, axis=-1)
            weights = jnp.where(allowed, jnp.exp(scores - row_peak[..., None]), 0.0)
            prob = weights / jnp.sum(weights, axis=-1)[..., None]
            dprob = jnp.einsum("qhd,kd->hqk", grad_rows, value_head)
            row_dot = jnp.sum(prob * dprob, axis=-1)
            dscore = round_half(prob * (tanh_gate * (dprob - row_dot[..., None])))
            prob_half = round_half(prob)
            query_part = jnp.einsum("hqk,kd->qhd", dscore, key_head)
            key_acc = state[0] + jnp.einsum("hqk,qhd->kd", dscore, query_rows)
            value_acc = state[1] + jnp.einsum("hqk,qhd->kd", prob_half, grad_rows)
            gate_acc = state[2] + jnp.sum(row_dot)
            return (key_acc, value_acc, gate_acc), query_part

        zero_rows = jnp.zeros((IMG, DH), jnp.float32)
        start_state = (zero_rows, zero_rows, jnp.zeros((), jnp.float32))
        (key_acc, value_acc, gate_acc), query_parts = lax.scan(one_block, start_state, jnp.arange(block_count, dtype=jnp.int32))
        return query_parts.reshape(SEQ, GROUP, DH), key_acc, value_acc, gate_acc

    query_acc, key_acc, value_acc, gate_acc = lax.map(per_head, (queries, cotangent, key_heads, value_heads))
    cross_query_grad = (query_acc.transpose(1, 0, 2, 3).reshape(SEQ, KVH * GROUP * DH) * score_scale).astype(jnp.bfloat16)
    image_key_grad = (key_acc.transpose(1, 0, 2).reshape(IMG, KVH * DH) * score_scale).astype(jnp.bfloat16)
    image_value_grad = (value_acc.transpose(1, 0, 2).reshape(IMG, KVH * DH) * tanh_gate).astype(jnp.bfloat16)
    gate_grad = ((1.0 - tanh_gate * tanh_gate) * jnp.sum(gate_acc)).reshape(1)
    return cross_query_grad, image_key_grad, image_value_grad, gate_grad


def reference(query_self, key_self, value_self, grad_self, document_id, query_cross, image_keys, image_values, grad_cross, image_block, gate, w_key, w_value):
    query_grad, key_grad, value_grad = self_attention(query_self, key_self, value_self, grad_self, document_id)
    input_part = jnp.dot(key_grad, w_key.T, preferred_element_type=jnp.float32)
    input_part = input_part + jnp.dot(value_grad, w_value.T, preferred_element_type=jnp.float32)
    input_grad = input_part.astype(jnp.bfloat16)
    tanh_gate = jnp.tanh(gate[0])
    cross_query_grad, image_key_grad, image_value_grad, gate_grad = cross_attention(query_cross, image_keys, image_values, grad_cross, image_block, tanh_gate)
    return (query_grad, key_grad, value_grad, input_grad, cross_query_grad, image_key_grad, image_value_grad, gate_grad)
```

```python
import functools
import math

import jax
import jax.numpy as jnp
from jax import lax
from jax.experimental import pallas as pl
from jax.experimental.pallas import tpu as pltpu
from jax.sharding import PartitionSpec as P

DH = 128
GROUP = 8
NIMG = 4
DOC_MAX = 2176

NEG_FILL = -1e30
SCALE = DH ** (-0.5)
LOG2E = math.log2(math.e)
KB = 256
PAIR = 256


def dot(a, b):
    return lax.dot_general(a, b, (((1,), (0,)), ((), ())), preferred_element_type=jnp.float32)


def attn_kernel(
    bounds_ref,
    gain_ref,
    low_ref,
    high_ref,
    q_ref,
    g_ref,
    k_ref,
    v_ref,
    dq_ref,
    dk_ref,
    dv_ref,
    dot_ref,
    e_s,
    d_s,
    peak_s,
    kt_s,
    qt_s,
    gt_s,
    qr_s,
    gr_s,
    dk_s,
    dv_s,
):
    first, clear0, clear1, last = bounds_ref[0], bounds_ref[1], bounds_ref[2], bounds_ref[3]
    gain = gain_ref[0]
    low = low_ref[...]
    high = high_ref[...]
    tok = q_ref.shape[0]
    for h in range(GROUP):
        p, o = (h * tok) // PAIR, (h * tok) % PAIR
        qh = q_ref[:, h * DH : (h + 1) * DH]
        gh = g_ref[:, h * DH : (h + 1) * DH]
        qr_s[p, o : o + tok, :] = qh
        gr_s[p, o : o + tok, :] = gh
        qt_s[p, :, o : o + tok] = qh.T
        gt_s[p, :, o : o + tok] = gh.T

    def prepare(b, carry):
        start = pl.multiple_of(b * KB, KB)
        kt_s[b - first] = k_ref[pl.ds(start, KB), :].T
        where = pl.multiple_of((b - first) * KB, KB)
        dk_s[pl.ds(where, KB), :] = jnp.zeros((KB, DH), jnp.float32)
        dv_s[pl.ds(where, KB), :] = jnp.zeros((KB, DH), jnp.float32)
        return carry

    lax.fori_loop(first, last, prepare, 0)

    def one_pair(p, dot_total):
        qt = qt_s[p]
        gt = gt_s[p]

        def stats(masked, b, carry):
            peak, total, dsum = carry
            start = pl.multiple_of(b * KB, KB)
            where = pl.multiple_of((b - first) * KB, KB)
            s = dot(k_ref[pl.ds(start, KB), :], qt) * (SCALE * LOG2E)
            dp = dot(v_ref[pl.ds(start, KB), :], gt)
            if masked:
                pos = start + lax.broadcasted_iota(jnp.int32, (KB, PAIR), 0)
                allowed = (pos >= low) & (pos <= high)
                s = jnp.where(allowed, s, NEG_FILL)
            new = jnp.maximum(peak, jnp.max(s, axis=0, keepdims=True))
            e = jnp.exp2(s - new)
            if masked:
                e = jnp.where(allowed, e, 0.0)
            factor = jnp.exp2(peak - new)
            e_s[pl.ds(where, KB), :] = e
            d_s[pl.ds(where, KB), :] = dp
            peak_s[b - first] = new
            total = total * factor + jnp.sum(e, axis=0, keepdims=True)
            dsum = dsum * factor + jnp.sum(e * dp, axis=0, keepdims=True)
            return new, total, dsum

        carry = (
            jnp.full((1, PAIR), NEG_FILL, jnp.float32),
            jnp.zeros((1, PAIR), jnp.float32),
            jnp.zeros((1, PAIR), jnp.float32),
        )
        carry = lax.fori_loop(first, clear0, functools.partial(stats, True), carry)
        carry = lax.fori_loop(clear0, clear1, functools.partial(stats, False), carry)
        peak, total, dsum = lax.fori_loop(clear1, last, functools.partial(stats, True), carry)
        inv = 1.0 / total
        delta = dsum * inv

        def grads(b, dqt):
            where = pl.multiple_of((b - first) * KB, KB)
            norm = jnp.exp2(peak_s[b - first] - peak) * inv
            prob = e_s[pl.ds(where, KB), :] * norm
            ds = (prob * (d_s[pl.ds(where, KB), :] - delta)).astype(jnp.bfloat16)
            dv_s[pl.ds(where, KB), :] += dot(prob.astype(jnp.bfloat16), gr_s[p])
            dk_s[pl.ds(where, KB), :] += dot(ds, qr_s[p])
            return dqt + dot(kt_s[b - first], ds)

        dqt = lax.fori_loop(first, last, grads, jnp.zeros((DH, PAIR), jnp.float32))
        dqt = dqt * (SCALE * gain)
        for i in range(PAIR // tok):
            at = pl.multiple_of(p * (PAIR // tok) * DH + i * DH, DH)
            dq_ref[:, pl.ds(at, DH)] = dqt[:, i * tok : (i + 1) * tok].T.astype(jnp.bfloat16)
        return dot_total + delta

    dot_ref[...] = lax.fori_loop(
        0, GROUP * tok // PAIR, one_pair, jnp.zeros((1, PAIR), jnp.float32)
    )
    dk_ref[...] = jnp.zeros(dk_ref.shape, dk_ref.dtype)
    dv_ref[...] = jnp.zeros(dv_ref.shape, dv_ref.dtype)

    def flush(b, carry):
        start = pl.multiple_of(b * KB, KB)
        where = pl.multiple_of((b - first) * KB, KB)
        dk_ref[pl.ds(start, KB), :] = (dk_s[pl.ds(where, KB), :] * (SCALE * gain)).astype(
            jnp.bfloat16
        )
        dv_ref[pl.ds(start, KB), :] = (dv_s[pl.ds(where, KB), :] * gain).astype(jnp.bfloat16)
        return carry

    lax.fori_loop(first, last, flush, 0)


def attention_grads(name, bounds, gain, low, high, q, g, k, v, max_blocks):
    tok = q.shape[0]
    keys = k.shape[0]
    pairs = GROUP * tok // PAIR
    smem = pl.BlockSpec(memory_space=pltpu.SMEM)
    vmem = pl.BlockSpec(memory_space=pltpu.VMEM)
    steps = max_blocks * KB
    flops = 10 * GROUP * tok * steps * DH
    return pl.pallas_call(
        attn_kernel,
        name=name,
        out_shape=(
            jax.ShapeDtypeStruct(q.shape, jnp.bfloat16),
            jax.ShapeDtypeStruct((keys, DH), jnp.bfloat16),
            jax.ShapeDtypeStruct((keys, DH), jnp.bfloat16),
            jax.ShapeDtypeStruct((1, PAIR), jnp.float32),
        ),
        in_specs=[smem, smem, vmem, vmem, vmem, vmem, vmem, vmem],
        out_specs=(vmem, vmem, vmem, vmem),
        scratch_shapes=[
            pltpu.VMEM((steps, PAIR), jnp.float32),
            pltpu.VMEM((steps, PAIR), jnp.float32),
            pltpu.VMEM((max_blocks, 1, PAIR), jnp.float32),
            pltpu.VMEM((max_blocks, DH, KB), jnp.bfloat16),
            pltpu.VMEM((pairs, DH, PAIR), jnp.bfloat16),
            pltpu.VMEM((pairs, DH, PAIR), jnp.bfloat16),
            pltpu.VMEM((pairs, PAIR, DH), jnp.bfloat16),
            pltpu.VMEM((pairs, PAIR, DH), jnp.bfloat16),
            pltpu.VMEM((steps, DH), jnp.float32),
            pltpu.VMEM((steps, DH), jnp.float32),
        ],
        cost_estimate=pl.CostEstimate(
            flops=flops,
            transcendentals=GROUP * tok * steps,
            bytes_accessed=2 * (3 * q.size + 4 * k.size),
        ),
        compiler_params=pltpu.CompilerParams(vmem_limit_bytes=32 * 1024 * 1024),
    )(bounds, gain, low, high, q, g, k, v)


def block_bounds(first_key, clear_from, clear_to, last_key):
    first = first_key // KB
    last = last_key // KB + 1
    clear0 = jnp.clip((clear_from + KB - 1) // KB, first, last)
    clear1 = jnp.clip((clear_to + 1) // KB, clear0, last)
    return jnp.stack([first, clear0, clear1, last]).astype(jnp.int32)


def local(
    query_self,
    key_self,
    value_self,
    grad_self,
    document_id,
    query_cross,
    image_keys,
    image_values,
    grad_cross,
    image_block,
    gate,
    w_key,
    w_value,
):
    rows = query_self.shape[0]
    seq_len = rows * lax.axis_size("ctx")
    first_row = lax.axis_index("ctx") * rows
    row_pos = first_row + jnp.arange(rows, dtype=jnp.int32)
    row_doc = lax.dynamic_slice_in_dim(document_id, first_row, rows, 0)
    low = jnp.sum(document_id[None, :] < row_doc[:, None], axis=1, dtype=jnp.int32)
    repeat = PAIR // rows

    def per_pair(row_values):
        return jnp.tile(row_values, repeat)[None, :]

    pair = lax.all_gather(
        jnp.stack([key_self, value_self]), "ctx", axis=1, tiled=True
    )
    image_pair = lax.all_gather(
        jnp.stack([image_keys, image_values]), "ctx", axis=1, tiled=True
    )
    one = jnp.ones((1,), jnp.float32)
    max_blocks = min((DOC_MAX - 1 + rows + KB - 2) // KB + 1, seq_len // KB)
    query_grad, key_part, value_part, _ = attention_grads(
        "self_attention",
        block_bounds(low[0], low[-1], first_row, first_row + rows - 1),
        one,
        per_pair(low),
        per_pair(row_pos),
        query_self,
        grad_self,
        pair[0],
        pair[1],
        max_blocks,
    )
    part = lax.psum_scatter(
        jnp.stack([key_part, value_part]), "ctx", scatter_dimension=1, tiled=True
    )
    key_grad, value_grad = part[0], part[1]

    tanh_gate = jnp.tanh(gate)
    image_total = image_pair.shape[1]
    image_len = image_total // NIMG
    limit = (image_block + 1) * image_len - 1
    cross_query_grad, image_key_part, image_value_part, row_dots = attention_grads(
        "cross_attention",
        block_bounds(jnp.int32(0), jnp.int32(0), limit[0], limit[-1]),
        tanh_gate,
        jnp.zeros((1, PAIR), jnp.int32),
        per_pair(limit),
        query_cross,
        grad_cross,
        image_pair[0],
        image_pair[1],
        image_total // KB,
    )
    input_part = dot(key_grad, w_key.T) + dot(value_grad, w_value.T)
    input_grad = lax.psum_scatter(
        input_part.astype(jnp.bfloat16), "tp", scatter_dimension=1, tiled=True
    )
    image_part = lax.psum_scatter(
        jnp.stack([image_key_part, image_value_part]), "ctx", scatter_dimension=1, tiled=True
    )
    gate_total = lax.psum(jnp.sum(row_dots), ("ctx", "tp"))
    gate_grad = (1.0 - tanh_gate * tanh_gate) * gate_total
    return (
        query_grad,
        key_grad,
        value_grad,
        input_grad,
        cross_query_grad,
        image_part[0],
        image_part[1],
        gate_grad,
    )


def solution(mesh):
    in_specs = (
        P("ctx", "tp"),
        P("ctx", "tp"),
        P("ctx", "tp"),
        P("ctx", "tp"),
        P(),
        P("ctx", "tp"),
        P("ctx", "tp"),
        P("ctx", "tp"),
        P("ctx", "tp"),
        P("ctx"),
        P(),
        P(None, "tp"),
        P(None, "tp"),
    )
    out_specs = (
        P("ctx", "tp"),
        P("ctx", "tp"),
        P("ctx", "tp"),
        P("ctx", "tp"),
        P("ctx", "tp"),
        P("ctx", "tp"),
        P("ctx", "tp"),
        P(),
    )
    return jax.shard_map(local, mesh=mesh, in_specs=in_specs, out_specs=out_specs, check_vma=False)
```

```python
import functools
import math

import jax
import jax.numpy as jnp
from jax import lax
from jax.experimental import pallas as pl
from jax.experimental.pallas import tpu as pltpu
from jax.sharding import PartitionSpec as P


DH = 128
GROUP = 8
NIMG = 4
DOCS = 16
DOC_MAX = 2176

NEG_FILL = -1e30
SCALE = DH ** (-0.5)
LOG2E = math.log2(math.e)
KB = 256
PAIR = 256
PAD = 16
NY, NZ, NCORE, NX = 4, 4, 2, 4

SMEM = pl.BlockSpec(memory_space=pltpu.SMEM)
VMEM = pl.BlockSpec(memory_space=pltpu.VMEM)
BF16 = jnp.bfloat16
F32 = jnp.float32


def shaped(shape, dtype):
    return jax.ShapeDtypeStruct(shape, dtype)


def dot(a, b):
    return lax.dot_general(a, b, (((1,), (0,)), ((), ())), preferred_element_type=F32)


def dot_t(a, b):
    return lax.dot_general(a, b, (((1,), (1,)), ((), ())), preferred_element_type=F32)


def ctx_shift(dy, dz, flip):
    def move(c):
        y, z, core = c // 8, (c // 2) % 4, c % 2
        return ((y + dy) % NY) * 8 + ((z + dz) % NZ) * 2 + (core ^ flip)

    return [(c, move(c)) for c in range(NY * NZ * NCORE)]


def send_y(value, k):
    return lax.ppermute(value, "ctx", ctx_shift(k, 0, 0))


def send_z(value, k):
    return lax.ppermute(value, "ctx", ctx_shift(0, k, 0))


def send_core(value):
    return lax.ppermute(value, "ctx", ctx_shift(0, 0, 1))


def send_x(value, k):
    perm = [(t, (t // NX) * NX + (t + k) % NX) for t in range(2 * NX)]
    return lax.ppermute(value, "tp", perm)


def send_zh(value):
    return lax.ppermute(value, "tp", [(t, t ^ NX) for t in range(2 * NX)])


def after(value, *earlier):
    return lax.optimization_barrier((value,) + earlier)[0]


def stack_kernel(k_ref, v_ref, ik_ref, iv_ref, kv_ref, ikv_ref):
    kv_ref[0] = k_ref[...]
    kv_ref[1] = v_ref[...]
    ikv_ref[0] = ik_ref[...]
    ikv_ref[1] = iv_ref[...]


def rows_kernel(
    ctx_ref, gate_ref, doc_ref, block_ref, low_ref, high_ref, limit_ref, gain_ref, bounds_ref
):
    tok = doc_ref.shape[1]
    c = ctx_ref[0]
    docs = doc_ref[...]
    mine = doc_ref[pl.ds(c, 1), :]
    low = jnp.zeros((1, tok), jnp.int32)
    for d in range(1, DOCS):
        before = jnp.sum((docs < d).astype(F32), axis=0, keepdims=True)
        before = jnp.sum(before, axis=1, keepdims=True).astype(jnp.int32)
        low = jnp.where(mine == d, before, low)
    high = c * tok + lax.broadcasted_iota(jnp.int32, (1, tok), 1)
    limit = (block_ref[...] + 1) * (bounds_scale(doc_ref) // NIMG) - 1
    for i in range(PAIR // tok):
        low_ref[:, i * tok : (i + 1) * tok] = low
        high_ref[:, i * tok : (i + 1) * tok] = high
        limit_ref[:, i * tok : (i + 1) * tok] = limit
    gain_ref[...] = jnp.tanh(jnp.full(gain_ref.shape, gate_ref[0], F32))
    shift = KB.bit_length() - 1

    def put(at, first_key, clear_from, clear_to, last_key):
        first = lax.shift_right_logical(first_key, shift)
        last = lax.shift_right_logical(last_key, shift) + 1
        clear0 = lax.shift_right_logical(clear_from + KB - 1, shift)
        clear0 = jnp.minimum(jnp.maximum(clear0, first), last)
        clear1 = lax.shift_right_logical(clear_to + 1, shift)
        clear1 = jnp.minimum(jnp.maximum(clear1, clear0), last)
        for i, value in enumerate((first, clear0, clear1, last)):
            bounds_ref[at + i] = value

    put(0, jnp.min(low), jnp.max(low), c * tok, c * tok + tok - 1)
    put(4, jnp.int32(0), jnp.int32(0), jnp.min(limit), jnp.max(limit))


def bounds_scale(doc_ref):
    return doc_ref.shape[0] * doc_ref.shape[1] // 2


def order_kernel(ctx_ref, *refs):
    out_ref = refs[-1]
    z = lax.shift_right_logical(ctx_ref[0], 1) & (NZ - 1)
    for k in range(NZ):
        out_ref[(z - k) & (NZ - 1)] = refs[k][...]


def weights_kernel(order_ref, wk_ref, wv_ref, *out_refs):
    step = pl.program_id(0)
    for k in range(NX):

        @pl.when(lax.shift_right_logical(step, 1) == k)
        def _():
            out_refs[k][0, 0] = wk_ref[...]
            out_refs[k][0, 1] = wv_ref[...]


def weight_pieces(tp, w_key, w_value):
    rows = w_key.shape[0] // (2 * NX)
    zh, x = tp // NX, tp % NX
    step = jnp.arange(2 * NX, dtype=jnp.int32)
    order = ((zh + (step & 1)) & 1) * NX + ((x + (step >> 1)) & (NX - 1))

    def piece_map(k):
        return lambda g, order: (jnp.clip(g - 2 * k, 0, 1), 0, 0, 0)

    return pl.pallas_call(
        weights_kernel,
        name="weight_pieces",
        grid_spec=pltpu.PrefetchScalarGridSpec(
            num_scalar_prefetch=1,
            grid=(2 * NX,),
            in_specs=[pl.BlockSpec((rows, DH), lambda g, order: (order[g], 0))] * 2,
            out_specs=[pl.BlockSpec((1, 2, rows, DH), piece_map(k)) for k in range(NX)],
        ),
        out_shape=[shaped((2, 2, rows, DH), BF16)] * NX,
    )(order, w_key, w_value)


def split_gate(total):
    hi = total.astype(BF16).astype(F32)
    mid = (total - hi).astype(BF16).astype(F32)
    lo = (total - hi) - mid
    row = lax.broadcasted_iota(jnp.int32, (PAD, DH), 0)
    rows = jnp.where(row == 0, hi, jnp.where(row == 1, mid, jnp.where(row == 2, lo, 0.0)))
    return rows.astype(BF16)


def join_gate(rows):
    return jnp.sum(rows.astype(F32), axis=0, keepdims=True)


def core_sum_kernel(pad, own_ref, other_ref, *out_refs):
    n = out_refs[0].shape[0] - pad
    if pad:
        at = NY * n
        tail = split_gate(join_gate(own_ref[at : at + pad]) + join_gate(other_ref[at : at + pad]))
    for k in range(NY):
        at = k * n
        total = own_ref[at : at + n].astype(F32) + other_ref[at : at + n].astype(F32)
        out_refs[k][0:n] = total.astype(BF16)
        if pad:
            out_refs[k][n : n + pad] = tail


def y_sum_kernel(pad, ctx_ref, s0_ref, s1_ref, s2_ref, s3_ref, *out_refs):
    n = out_refs[0].shape[0] - pad
    z = lax.shift_right_logical(ctx_ref[0], 1) & (NZ - 1)
    ins = (s0_ref, s1_ref, s2_ref, s3_ref)
    if pad:
        tail = split_gate(sum(join_gate(r[NZ * n : NZ * n + pad]) for r in ins))
    for k in range(NZ):
        at = pl.multiple_of(((z + k) & (NZ - 1)) * n, n)
        total = sum(r[pl.ds(at, n)].astype(F32) for r in ins)
        out_refs[k][0:n] = total.astype(BF16)
        if pad:
            out_refs[k][n : n + pad] = tail


def z_sum_kernel(pad, s0_ref, s1_ref, s2_ref, s3_ref, *out_refs):
    ins = (s0_ref, s1_ref, s2_ref, s3_ref)
    n = ins[0].shape[0] - pad
    total = sum(r[0:n].astype(F32) for r in ins).astype(BF16)
    if pad:
        gate = sum(join_gate(r[n : n + pad]) for r in ins)
        out_refs[2][...] = jnp.broadcast_to(gate, out_refs[2].shape)
    else:
        out_refs[2][...] = total
    out_refs[0][...] = total[: n // 2]
    out_refs[1][...] = total[n // 2 :]


def project_kernel(*refs):
    grads, weights, out_ref = refs[:NX], refs[NX : 2 * NX], refs[2 * NX]
    tok = grads[0].shape[0] // 2
    cols = 256
    for j in range(out_ref.shape[1] // cols):
        total = None
        for g, w in zip(grads, weights):
            for i in range(2):
                part = dot_t(g[i * tok : (i + 1) * tok], w[0, i, j * cols : (j + 1) * cols])
                total = part if total is None else total + part
        out_ref[:, j * cols : (j + 1) * cols] = total.astype(out_ref.dtype)


def project(half, grads, weights):
    tok = grads[0].shape[0] // 2
    rows = weights[0].shape[2]
    return pl.pallas_call(
        project_kernel,
        grid=(1,),
        in_specs=[pl.BlockSpec(g.shape, lambda i: (0, 0)) for g in grads]
        + [pl.BlockSpec((1, 2, rows, DH), lambda i: (half, 0, 0, 0))] * NX,
        out_specs=pl.BlockSpec((tok, rows), lambda i: (0, 0)),
        out_shape=shaped((tok, rows), BF16 if half == 1 else F32),
        cost_estimate=pl.CostEstimate(
            flops=4 * NX * tok * rows * DH, transcendentals=0, bytes_accessed=4 * NX * rows * DH
        ),
    )(*grads, *weights)


def add_kernel(a_ref, b_ref, o_ref):
    o_ref[...] = (a_ref[...] + b_ref[...].astype(F32)).astype(o_ref.dtype)


def gate_sum_kernel(g0, g1, g2, g3, o_ref):
    o_ref[...] = g0[...] + g1[...] + g2[...] + g3[...]


def gate_out_kernel(a_ref, b_ref, gain_ref, o_ref):
    t = gain_ref[0:1, 0:DH]
    o_ref[...] = (1.0 - t * t) * (a_ref[0:1] + b_ref[0:1])


def call(kernel, outs, *args, smem=0):
    single = not isinstance(outs, (list, tuple))
    specs = [SMEM] * smem + [VMEM] * (len(args) - smem)
    return pl.pallas_call(
        kernel, out_shape=outs, in_specs=specs, out_specs=VMEM if single else [VMEM] * len(outs)
    )(*args)


def attn_kernel(block_rows, base, pad, *refs):
    ctx_ref, bounds_ref, low_ref, high_ref, gain_ref, q_ref, g_ref = refs[:7]
    mine, others = refs[7 : 7 + NY], refs[7 + NY : 7 + 2 * NY]
    dq_ref, own_ref, oth_ref = refs[7 + 2 * NY : 10 + 2 * NY]
    (k_s, v_s, e_s, d_s, peak_s, kt_s, qt_s, gt_s, qr_s, gr_s, dk_s, dv_s) = refs[10 + 2 * NY :]
    first, clear0, clear1, last = (bounds_ref[base + i] for i in range(4))
    c = ctx_ref[0]
    core, my_y = c & 1, lax.shift_right_logical(c, 3)
    gain = gain_ref[0:1, 0:DH]
    low = low_ref[...]
    high = high_ref[...]
    tok = q_ref.shape[0]

    for h in range(GROUP):
        p, o = (h * tok) // PAIR, (h * tok) % PAIR
        qh = q_ref[:, h * DH : (h + 1) * DH]
        gh = g_ref[:, h * DH : (h + 1) * DH]
        qr_s[p, o : o + tok, :] = qh
        gr_s[p, o : o + tok, :] = gh
        qt_s[p, :, o : o + tok] = qh.T
        gt_s[p, :, o : o + tok] = gh.T
    for k in range(NY):
        for flip, ref in ((0, mine[k]), (1, others[k])):
            for z in range(NZ):
                block = ((my_y - k) & (NY - 1)) * 8 + z * 2 + (core ^ flip)
                at = pl.multiple_of(block * block_rows, block_rows)
                k_s[pl.ds(at, block_rows), :] = ref[z, 0]
                v_s[pl.ds(at, block_rows), :] = ref[z, 1]

    def prepare(b, carry):
        start = pl.multiple_of(b * KB, KB)
        kt_s[b - first] = k_s[pl.ds(start, KB), :].T
        where = pl.multiple_of((b - first) * KB, KB)
        dk_s[pl.ds(where, KB), :] = jnp.zeros((KB, DH), F32)
        dv_s[pl.ds(where, KB), :] = jnp.zeros((KB, DH), F32)
        return carry

    lax.fori_loop(first, last, prepare, 0)

    def one_pair(p, dot_total):
        qt = qt_s[p]
        gt = gt_s[p]

        def stats(masked, b, carry):
            peak, total, dsum = carry
            start = pl.multiple_of(b * KB, KB)
            where = pl.multiple_of((b - first) * KB, KB)
            s = dot(k_s[pl.ds(start, KB), :], qt) * (SCALE * LOG2E)
            dp = dot(v_s[pl.ds(start, KB), :], gt)
            if masked:
                pos = start + lax.broadcasted_iota(jnp.int32, (KB, PAIR), 0)
                allowed = (pos >= low) & (pos <= high)
                s = jnp.where(allowed, s, NEG_FILL)
            new = jnp.maximum(peak, jnp.max(s, axis=0, keepdims=True))
            e = jnp.exp2(s - new)
            if masked:
                e = jnp.where(allowed, e, 0.0)
            factor = jnp.exp2(peak - new)
            e_s[pl.ds(where, KB), :] = e
            d_s[pl.ds(where, KB), :] = dp
            peak_s[b - first] = new
            total = total * factor + jnp.sum(e, axis=0, keepdims=True)
            dsum = dsum * factor + jnp.sum(e * dp, axis=0, keepdims=True)
            return new, total, dsum

        carry = (
            jnp.full((1, PAIR), NEG_FILL, F32),
            jnp.zeros((1, PAIR), F32),
            jnp.zeros((1, PAIR), F32),
        )
        carry = lax.fori_loop(first, clear0, functools.partial(stats, True), carry)
        carry = lax.fori_loop(clear0, clear1, functools.partial(stats, False), carry)
        peak, total, dsum = lax.fori_loop(clear1, last, functools.partial(stats, True), carry)
        inv = 1.0 / total
        delta = dsum * inv

        def grads(b, dqt):
            where = pl.multiple_of((b - first) * KB, KB)
            norm = jnp.exp2(peak_s[b - first] - peak) * inv
            prob = e_s[pl.ds(where, KB), :] * norm
            ds = (prob * (d_s[pl.ds(where, KB), :] - delta)).astype(BF16)
            dv_s[pl.ds(where, KB), :] += dot(prob.astype(BF16), gr_s[p])
            dk_s[pl.ds(where, KB), :] += dot(ds, qr_s[p])
            return dqt + dot(kt_s[b - first], ds)

        dqt = lax.fori_loop(first, last, grads, jnp.zeros((DH, PAIR), F32))
        for i in range(PAIR // tok):
            at = pl.multiple_of(p * (PAIR // tok) * DH + i * DH, DH)
            part = dqt[:, i * tok : (i + 1) * tok] * (gain * SCALE)
            dq_ref[:, pl.ds(at, DH)] = part.T.astype(BF16)
        return dot_total + delta

    dots = lax.fori_loop(0, GROUP * tok // PAIR, one_pair, jnp.zeros((1, PAIR), F32))

    n = NZ * 2 * block_rows
    own_ref[...] = jnp.zeros(own_ref.shape, own_ref.dtype)
    oth_ref[...] = jnp.zeros(oth_ref.shape, oth_ref.dtype)
    per_step = KB // block_rows

    def flush(b, carry):
        for i in range(per_step):
            block = b * per_step + i
            k = (lax.shift_right_logical(block, 3) - my_y) & (NY - 1)
            z = lax.shift_right_logical(block, 1) & (NZ - 1)
            at = pl.multiple_of(k * n + z * 2 * block_rows, block_rows)
            where = pl.multiple_of((b - first) * KB + i * block_rows, block_rows)
            dk = (dk_s[pl.ds(where, block_rows), :] * (gain * SCALE)).astype(BF16)
            dv = (dv_s[pl.ds(where, block_rows), :] * gain).astype(BF16)
            for same, ref in ((True, own_ref), (False, oth_ref)):

                @pl.when((core == (i & 1)) if same else (core != (i & 1)))
                def _():
                    ref[pl.ds(at, block_rows), :] = dk
                    ref[pl.ds(at + block_rows, block_rows), :] = dv

        return carry

    lax.fori_loop(first, last, flush, 0)
    if pad:
        gate = jnp.broadcast_to(jnp.sum(dots, axis=1, keepdims=True), (1, DH))
        own_ref[NY * n : NY * n + pad] = split_gate(gate)
        oth_ref[NY * n : NY * n + pad] = split_gate(gate)


def attention_grads(base, pad, max_blocks, ctx, bounds, low, high, gain, q, g, mine, others):
    tok = q.shape[0]
    block_rows = mine[0].shape[2]
    keys = NY * NZ * NCORE * block_rows
    pairs = GROUP * tok // PAIR
    steps = max_blocks * KB
    half = shaped((keys + pad, DH), BF16)
    return pl.pallas_call(
        functools.partial(attn_kernel, block_rows, base, pad),
        out_shape=(shaped(q.shape, BF16), half, half),
        in_specs=[SMEM, SMEM] + [VMEM] * (5 + 2 * NY),
        out_specs=(VMEM, VMEM, VMEM),
        scratch_shapes=[
            pltpu.VMEM((keys, DH), BF16),
            pltpu.VMEM((keys, DH), BF16),
            pltpu.VMEM((steps, PAIR), F32),
            pltpu.VMEM((steps, PAIR), F32),
            pltpu.VMEM((max_blocks, 1, PAIR), F32),
            pltpu.VMEM((max_blocks, DH, KB), BF16),
            pltpu.VMEM((pairs, DH, PAIR), BF16),
            pltpu.VMEM((pairs, DH, PAIR), BF16),
            pltpu.VMEM((pairs, PAIR, DH), BF16),
            pltpu.VMEM((pairs, PAIR, DH), BF16),
            pltpu.VMEM((steps, DH), F32),
            pltpu.VMEM((steps, DH), F32),
        ],
        cost_estimate=pl.CostEstimate(
            flops=10 * GROUP * tok * steps * DH,
            transcendentals=GROUP * tok * steps,
            bytes_accessed=2 * (3 * q.size + 4 * keys * DH),
        ),
        compiler_params=pltpu.CompilerParams(vmem_limit_bytes=32 * 1024 * 1024),
    )(ctx, bounds, low, high, gain, q, g, *mine, *others)


def local(
    query_self,
    key_self,
    value_self,
    grad_self,
    document_id,
    query_cross,
    image_keys,
    image_values,
    grad_cross,
    image_block,
    gate,
    w_key,
    w_value,
):
    tok = query_self.shape[0]
    img = image_keys.shape[0]
    seq = document_id.shape[0]
    ctx = lax.axis_index("ctx").reshape(1)
    tp = lax.axis_index("tp")

    kv, ikv = call(
        stack_kernel,
        (shaped((2, tok, DH), BF16), shaped((2, img, DH), BF16)),
        key_self,
        value_self,
        image_keys,
        image_values,
    )
    kv_z = [kv] + [send_z(kv, k) for k in range(1, NZ)]
    rows_doc = after(document_id.reshape(seq // tok, tok), kv)
    low, high, limit, gain, bounds = pl.pallas_call(
        rows_kernel,
        name="rows",
        out_shape=(shaped((1, PAIR), jnp.int32),) * 3
        + (shaped((8, DH), F32), shaped((8,), jnp.int32)),
        in_specs=[SMEM, SMEM, VMEM, VMEM],
        out_specs=(VMEM,) * 4 + (SMEM,),
    )(ctx, gate, rows_doc, image_block.reshape(1, tok))
    kv_mine = call(order_kernel, shaped((NZ, 2, tok, DH), BF16), ctx, *kv_z, smem=1)
    pieces = weight_pieces(after(tp, kv_mine), w_key, w_value)
    ikv = after(ikv, kv_mine)
    ikv_z = [ikv] + [send_z(ikv, k) for k in range(1, NZ)]
    mine = [kv_mine] + [send_y(kv_mine, k) for k in range(1, NY)]
    others = [send_core(m) for m in mine]
    weights = [pieces[0]] + [send_x(pieces[k], k) for k in range(1, NX)]
    ikv_mine = call(order_kernel, shaped((NZ, 2, img, DH), BF16), ctx, *ikv_z, smem=1)
    imine = [ikv_mine] + [send_y(ikv_mine, k) for k in range(1, NY)]
    query = after(query_self, ikv_mine)

    ones = jnp.ones((8, DH), F32)
    max_blocks = min((DOC_MAX - 1 + tok + KB - 2) // KB + 1, seq // KB)
    query_grad, own, other = attention_grads(
        0, 0, max_blocks, ctx, bounds, low, high, ones, query, grad_self, mine, others
    )
    got = send_core(other)
    imine = [after(m, own) for m in imine]
    iothers = [send_core(m) for m in imine]
    piece = shaped((NZ * 2 * tok, DH), BF16)
    share = call(functools.partial(core_sum_kernel, 0), [piece] * NY, own, got)
    query = after(query_cross, share[0])
    share = [share[0]] + [send_y(share[k], k) for k in range(1, NY)]
    cross_query_grad, iown, iother = attention_grads(
        4,
        PAD,
        seq // 2 // KB,
        ctx,
        bounds,
        jnp.zeros((1, PAIR), jnp.int32),
        limit,
        gain,
        query,
        grad_cross,
        imine,
        iothers,
    )
    igot = send_core(iother)
    piece = shaped((2 * tok, DH), BF16)
    share[0] = after(share[0], iown, *weights[1:])
    share = call(functools.partial(y_sum_kernel, 0), [piece] * NZ, ctx, *share, smem=1)
    iown = after(iown, share[0])
    share = [share[0]] + [send_z(share[k], k) for k in range(1, NZ)]
    ipiece = shaped((NZ * 2 * img + PAD, DH), BF16)
    ishare = call(functools.partial(core_sum_kernel, PAD), [ipiece] * NY, iown, igot)
    share[0] = after(share[0], ishare[0])
    ishare = [ishare[0]] + [send_y(ishare[k], k) for k in range(1, NY)]
    one = shaped((tok, DH), BF16)
    key_grad, value_grad, both = call(functools.partial(z_sum_kernel, 0), [one, one, piece], *share)
    ishare[0] = after(ishare[0], both)
    both = [both] + [send_x(both, k) for k in range(1, NX)]
    ipiece = shaped((2 * img + PAD, DH), BF16)
    ishare = call(functools.partial(y_sum_kernel, PAD), [ipiece] * NZ, ctx, *ishare, smem=1)
    both[0] = after(both[0], ishare[0])
    ishare = [ishare[0]] + [send_z(ishare[k], k) for k in range(1, NZ)]
    away = project(1, both, weights)
    both[0] = after(both[0], away)
    ishare[0] = after(ishare[0], away)
    away = send_zh(away)
    home = project(0, both, weights)
    one = shaped((img, DH), BF16)
    gates = shaped((8, DH), F32)
    image_key_grad, image_value_grad, total = call(
        functools.partial(z_sum_kernel, PAD), [one, one, gates], *ishare
    )
    total = [total] + [send_x(total, k) for k in range(1, NX)]
    total = call(gate_sum_kernel, gates, *total)
    far = send_zh(total)
    input_grad = call(add_kernel, shaped(home.shape, BF16), home, away)
    gate_grad = call(gate_out_kernel, shaped((1, DH), F32), total, far, gain)
    return (
        query_grad,
        key_grad,
        value_grad,
        input_grad,
        cross_query_grad,
        image_key_grad,
        image_value_grad,
        gate_grad[0, :1],
    )


def solution(mesh):
    two = P("ctx", "tp")
    in_specs = (two,) * 4 + (P(),) + (two,) * 4 + (P("ctx"), P(), P(None, "tp"), P(None, "tp"))
    out_specs = (two,) * 7 + (P(),)


    return jax.shard_map(local, mesh=mesh, in_specs=in_specs, out_specs=out_specs, check_vma=False)
```

```python
import functools
import math

import jax
import jax.numpy as jnp
from jax import lax
from jax.experimental import pallas as pl
from jax.experimental.pallas import tpu as pltpu
from jax.sharding import PartitionSpec as P


DH = 128
GROUP = 8
NIMG = 4
DOCS = 16
DOC_MAX = 2176

NEG_FILL = -1e30
SCALE = DH ** (-0.5)
LOG2E = math.log2(math.e)
KB = 256
PAIR = 1024
PAD = 16
NY, NZ, NCORE, NX = 4, 4, 2, 4

SMEM = pl.BlockSpec(memory_space=pltpu.SMEM)
VMEM = pl.BlockSpec(memory_space=pltpu.VMEM)
BF16 = jnp.bfloat16
F32 = jnp.float32

SMALL = pltpu.CompilerParams(vmem_limit_bytes=8 * 1024 * 1024)


def shaped(shape, dtype):
    return jax.ShapeDtypeStruct(shape, dtype)


def dot(a, b):
    return lax.dot_general(a, b, (((1,), (0,)), ((), ())), preferred_element_type=F32)


def dot_t(a, b):
    return lax.dot_general(a, b, (((1,), (1,)), ((), ())), preferred_element_type=F32)


def ctx_shift(dy, dz, flip):
    def move(c):
        y, z, core = c // 8, (c // 2) % 4, c % 2
        return ((y + dy) % NY) * 8 + ((z + dz) % NZ) * 2 + (core ^ flip)

    return [(c, move(c)) for c in range(NY * NZ * NCORE)]


def send_y(value, k):
    return lax.ppermute(value, "ctx", ctx_shift(k, 0, 0))


def send_z(value, k):
    return lax.ppermute(value, "ctx", ctx_shift(0, k, 0))


def send_core(value):
    return lax.ppermute(value, "ctx", ctx_shift(0, 0, 1))


def send_x(value, k, flip=0):
    perm = [(t, ((t // NX) ^ flip) * NX + (t + k) % NX) for t in range(2 * NX)]
    return lax.ppermute(value, "tp", perm)


def send_zh(value):
    return lax.ppermute(value, "tp", [(t, t ^ NX) for t in range(2 * NX)])


def after(value, *earlier):
    return lax.optimization_barrier((value,) + earlier)[0]


def stack_kernel(k_ref, v_ref, ik_ref, iv_ref, kv_ref, ikv_ref):
    kv_ref[0] = k_ref[...]
    kv_ref[1] = v_ref[...]
    ikv_ref[0] = ik_ref[...]
    ikv_ref[1] = iv_ref[...]


def rows_kernel(
    ctx_ref, gate_ref, doc_ref, block_ref, low_ref, high_ref, limit_ref, gain_ref, bounds_ref
):
    tok = doc_ref.shape[1]
    c = ctx_ref[0]
    docs = doc_ref[...]
    mine = doc_ref[pl.ds(c, 1), :]
    low = jnp.zeros((1, tok), jnp.int32)
    for d in range(1, DOCS):
        before = jnp.sum((docs < d).astype(F32), axis=0, keepdims=True)
        before = jnp.sum(before, axis=1, keepdims=True).astype(jnp.int32)
        low = jnp.where(mine == d, before, low)
    high = c * tok + lax.broadcasted_iota(jnp.int32, (1, tok), 1)
    limit = (block_ref[...] + 1) * (bounds_scale(doc_ref) // NIMG) - 1
    for i in range(PAIR // tok):
        low_ref[:, i * tok : (i + 1) * tok] = low
        high_ref[:, i * tok : (i + 1) * tok] = high
        limit_ref[:, i * tok : (i + 1) * tok] = limit
    gain_ref[...] = jnp.tanh(jnp.full(gain_ref.shape, gate_ref[0], F32))
    shift = KB.bit_length() - 1

    def put(at, first_key, clear_from, clear_to, last_key):
        first = lax.shift_right_logical(first_key, shift)
        last = lax.shift_right_logical(last_key, shift) + 1
        clear0 = lax.shift_right_logical(clear_from + KB - 1, shift)
        clear0 = jnp.minimum(jnp.maximum(clear0, first), last)
        clear1 = lax.shift_right_logical(clear_to + 1, shift)
        clear1 = jnp.minimum(jnp.maximum(clear1, clear0), last)
        for i, value in enumerate((first, clear0, clear1, last)):
            bounds_ref[at + i] = value

    put(0, jnp.min(low), jnp.max(low), c * tok, c * tok + tok - 1)
    put(4, jnp.int32(0), jnp.int32(0), jnp.min(limit), jnp.max(limit))


def bounds_scale(doc_ref):
    return doc_ref.shape[0] * doc_ref.shape[1] // 2


def order_kernel(ctx_ref, *refs):
    out_ref = refs[-1]
    z = lax.shift_right_logical(ctx_ref[0], 1) & (NZ - 1)
    for k in range(NZ):
        out_ref[(z - k) & (NZ - 1)] = refs[k][...]


def merge_kernel(*refs):
    for k in range(NY):
        refs[-1][k] = refs[k][...]


def weights_kernel(order_ref, wk_ref, wv_ref, *out_refs):
    step = pl.program_id(0)
    for k in range(NX):

        @pl.when(lax.shift_right_logical(step, 1) == k)
        def _():
            out_refs[k][0, 0] = wk_ref[...]
            out_refs[k][0, 1] = wv_ref[...]


def weight_pieces(tp, w_key, w_value):
    rows = w_key.shape[0] // (2 * NX)
    zh, x = tp // NX, tp % NX
    step = jnp.arange(2 * NX, dtype=jnp.int32)
    order = ((zh + (step & 1)) & 1) * NX + ((x + (step >> 1)) & (NX - 1))

    def piece_map(k):
        return lambda g, order: (jnp.clip(g - 2 * k, 0, 1), 0, 0, 0)

    return pl.pallas_call(
        weights_kernel,
        name="weight_pieces",
        grid_spec=pltpu.PrefetchScalarGridSpec(
            num_scalar_prefetch=1,
            grid=(2 * NX,),
            in_specs=[pl.BlockSpec((rows, DH), lambda g, order: (order[g], 0))] * 2,
            out_specs=[pl.BlockSpec((1, 2, rows, DH), piece_map(k)) for k in range(NX)],
        ),
        out_shape=[shaped((2, 2, rows, DH), BF16)] * NX,
        compiler_params=pltpu.CompilerParams(vmem_limit_bytes=16 * 1024 * 1024),
    )(order, w_key, w_value)


def split_gate(total):
    hi = total.astype(BF16).astype(F32)
    mid = (total - hi).astype(BF16).astype(F32)
    lo = (total - hi) - mid
    row = lax.broadcasted_iota(jnp.int32, (PAD, DH), 0)
    rows = jnp.where(row == 0, hi, jnp.where(row == 1, mid, jnp.where(row == 2, lo, 0.0)))
    return rows.astype(BF16)


def join_gate(rows):
    return jnp.sum(rows.astype(F32), axis=0, keepdims=True)


def core_sum_kernel(pad, own_ref, other_ref, *out_refs):
    n = out_refs[0].shape[0] - pad
    if pad:
        at = NY * n
        tail = split_gate(join_gate(own_ref[at : at + pad]) + join_gate(other_ref[at : at + pad]))
    for k in range(NY):
        at = k * n
        total = own_ref[at : at + n].astype(F32) + other_ref[at : at + n].astype(F32)
        out_refs[k][0:n] = total.astype(BF16)
        if pad:
            out_refs[k][n : n + pad] = tail


def y_sum_kernel(pad, ctx_ref, s0_ref, s1_ref, s2_ref, s3_ref, *out_refs):
    n = out_refs[0].shape[0] - pad
    z = lax.shift_right_logical(ctx_ref[0], 1) & (NZ - 1)
    ins = (s0_ref, s1_ref, s2_ref, s3_ref)
    if pad:
        tail = split_gate(sum(join_gate(r[NZ * n : NZ * n + pad]) for r in ins))
    for k in range(NZ):
        at = pl.multiple_of(((z + k) & (NZ - 1)) * n, n)
        total = sum(r[pl.ds(at, n)].astype(F32) for r in ins)
        out_refs[k][0:n] = total.astype(BF16)
        if pad:
            out_refs[k][n : n + pad] = tail


def z_sum_kernel(pad, s0_ref, s1_ref, s2_ref, s3_ref, *out_refs):
    ins = (s0_ref, s1_ref, s2_ref, s3_ref)
    n = ins[0].shape[0] - pad
    total = sum(r[0:n].astype(F32) for r in ins).astype(BF16)
    if pad:
        gate = sum(join_gate(r[n : n + pad]) for r in ins)
        out_refs[2][...] = jnp.broadcast_to(gate, out_refs[2].shape)
    else:
        out_refs[2][...] = total
    out_refs[0][...] = total[: n // 2]
    out_refs[1][...] = total[n // 2 :]


def project_kernel(half, *refs):
    grads, weights, out_ref = refs[:NX], refs[NX : 2 * NX], refs[2 * NX]
    tok = grads[0].shape[0] // 2
    cols = 256
    for j in range(out_ref.shape[1] // cols):
        total = None
        for g, w in zip(grads, weights):
            for i in range(2):
                part = dot_t(g[i * tok : (i + 1) * tok], w[half, i, j * cols : (j + 1) * cols])
                total = part if total is None else total + part
        out_ref[:, j * cols : (j + 1) * cols] = total.astype(out_ref.dtype)


def project(half, grads, weights):
    tok = grads[0].shape[0] // 2
    rows = weights[0].shape[2]
    return pl.pallas_call(
        functools.partial(project_kernel, half),
        in_specs=[VMEM] * (2 * NX),
        out_specs=VMEM,
        compiler_params=pltpu.CompilerParams(vmem_limit_bytes=16 * 1024 * 1024),
        out_shape=shaped((tok, rows), BF16 if half == 1 else F32),
        cost_estimate=pl.CostEstimate(
            flops=4 * NX * tok * rows * DH, transcendentals=0, bytes_accessed=4 * NX * rows * DH
        ),
    )(*grads, *weights)


def gate_sum_kernel(g0, g1, g2, g3, o_ref):
    o_ref[...] = g0[...] + g1[...] + g2[...] + g3[...]


def finish_kernel(gain_ref, near_ref, far_ref, home_ref, away_ref, gate_ref, out_ref):
    t = gain_ref[0:1, 0:DH]
    gate_ref[...] = (1.0 - t * t) * (near_ref[0:1] + far_ref[0:1])
    out_ref[...] = (home_ref[...] + away_ref[...].astype(F32)).astype(out_ref.dtype)


def call(kernel, outs, *args, smem=0, params=SMALL):
    single = not isinstance(outs, (list, tuple))
    specs = [SMEM] * smem + [VMEM] * (len(args) - smem)
    return pl.pallas_call(
        kernel,
        out_shape=outs,
        in_specs=specs,
        out_specs=VMEM if single else [VMEM] * len(outs),
        compiler_params=params,
    )(*args)


def attn_kernel(block_rows, base, pad, merged, *refs):
    ctx_ref, bounds_ref, low_ref, high_ref, gain_ref, q_ref, g_ref = refs[:7]
    if merged:
        mine, others = ([ref.at[k] for k in range(NY)] for ref in refs[7:9])
        refs = refs[9:]
    else:
        mine, others = refs[7 : 7 + NY], refs[7 + NY : 7 + 2 * NY]
        refs = refs[7 + 2 * NY :]
    dq_ref, own_ref, oth_ref = refs[:3]
    (k_s, v_s, e_s, d_s, peak_s, kt_s, qt_s, gt_s, qr_s, gr_s, dk_s, dv_s) = refs[3:]
    first, clear0, clear1, last = (bounds_ref[base + i] for i in range(4))
    c = ctx_ref[0]
    core, my_y = c & 1, lax.shift_right_logical(c, 3)
    gain = gain_ref[0:1, 0:DH]
    low = low_ref[...]
    high = high_ref[...]
    tok = q_ref.shape[0]

    for h in range(GROUP):
        p, o = (h * tok) // PAIR, (h * tok) % PAIR
        qh = q_ref[:, h * DH : (h + 1) * DH]
        gh = g_ref[:, h * DH : (h + 1) * DH]
        qr_s[p, o : o + tok, :] = qh
        gr_s[p, o : o + tok, :] = gh
        qt_s[p, :, o : o + tok] = qh.T
        gt_s[p, :, o : o + tok] = gh.T
    for k in range(NY):
        for flip, ref in ((0, mine[k]), (1, others[k])):
            for z in range(NZ):
                block = ((my_y - k) & (NY - 1)) * 8 + z * 2 + (core ^ flip)
                at = pl.multiple_of(block * block_rows, block_rows)
                k_s[pl.ds(at, block_rows), :] = ref[z, 0]
                v_s[pl.ds(at, block_rows), :] = ref[z, 1]

    def prepare(b, carry):
        start = pl.multiple_of(b * KB, KB)
        kt_s[b - first] = k_s[pl.ds(start, KB), :].T
        where = pl.multiple_of((b - first) * KB, KB)
        dk_s[pl.ds(where, KB), :] = jnp.zeros((KB, DH), F32)
        dv_s[pl.ds(where, KB), :] = jnp.zeros((KB, DH), F32)
        return carry

    lax.fori_loop(first, last, prepare, 0)

    def one_pair(p, dot_total):
        qt = qt_s[p]
        gt = gt_s[p]

        def stats(masked, b, carry):
            peak, total, dsum = carry
            start = pl.multiple_of(b * KB, KB)
            where = pl.multiple_of((b - first) * KB, KB)
            s = dot(k_s[pl.ds(start, KB), :], qt) * (SCALE * LOG2E)
            dp = dot(v_s[pl.ds(start, KB), :], gt)
            if masked:
                pos = start + lax.broadcasted_iota(jnp.int32, (KB, PAIR), 0)
                allowed = (pos >= low) & (pos <= high)
                s = jnp.where(allowed, s, NEG_FILL)
            new = jnp.maximum(peak, jnp.max(s, axis=0, keepdims=True))
            e = jnp.exp2(s - new)
            if masked:
                e = jnp.where(allowed, e, 0.0)
            factor = jnp.exp2(peak - new)
            e_s[pl.ds(where, KB), :] = e
            d_s[pl.ds(where, KB), :] = dp
            peak_s[b - first] = new
            total = total * factor + jnp.sum(e, axis=0, keepdims=True)
            dsum = dsum * factor + jnp.sum(e * dp, axis=0, keepdims=True)
            return new, total, dsum

        carry = (
            jnp.full((1, PAIR), NEG_FILL, F32),
            jnp.zeros((1, PAIR), F32),
            jnp.zeros((1, PAIR), F32),
        )

        def edge(i, carry):
            b = first + i
            return stats(True, jnp.where(b < clear0, b, b + (clear1 - clear0)), carry)

        carry = lax.fori_loop(0, (last - first) - (clear1 - clear0), edge, carry)
        peak, total, dsum = lax.fori_loop(
            clear0, clear1, functools.partial(stats, False), carry
        )
        inv = 1.0 / total
        delta = dsum * inv

        def grads(b, dqt):
            where = pl.multiple_of((b - first) * KB, KB)
            norm = jnp.exp2(peak_s[b - first] - peak) * inv
            prob = e_s[pl.ds(where, KB), :] * norm
            ds = (prob * (d_s[pl.ds(where, KB), :] - delta)).astype(BF16)
            dv_s[pl.ds(where, KB), :] += dot(prob.astype(BF16), gr_s[p])
            dk_s[pl.ds(where, KB), :] += dot(ds, qr_s[p])
            return dqt + dot(kt_s[b - first], ds)

        dqt = lax.fori_loop(first, last, grads, jnp.zeros((DH, PAIR), F32))
        for i in range(PAIR // tok):
            at = pl.multiple_of(p * (PAIR // tok) * DH + i * DH, DH)
            part = dqt[:, i * tok : (i + 1) * tok] * (gain * SCALE)
            dq_ref[:, pl.ds(at, DH)] = part.T.astype(BF16)
        return dot_total + delta

    dots = lax.fori_loop(0, GROUP * tok // PAIR, one_pair, jnp.zeros((1, PAIR), F32))

    n = NZ * 2 * block_rows
    own_ref[...] = jnp.zeros(own_ref.shape, own_ref.dtype)
    oth_ref[...] = jnp.zeros(oth_ref.shape, oth_ref.dtype)
    per_step = KB // block_rows

    def flush(b, carry):
        for i in range(per_step):
            block = b * per_step + i
            k = (lax.shift_right_logical(block, 3) - my_y) & (NY - 1)
            z = lax.shift_right_logical(block, 1) & (NZ - 1)
            at = pl.multiple_of(k * n + z * 2 * block_rows, block_rows)
            where = pl.multiple_of((b - first) * KB + i * block_rows, block_rows)
            dk = (dk_s[pl.ds(where, block_rows), :] * (gain * SCALE)).astype(BF16)
            dv = (dv_s[pl.ds(where, block_rows), :] * gain).astype(BF16)
            for same, ref in ((True, own_ref), (False, oth_ref)):

                @pl.when((core == (i & 1)) if same else (core != (i & 1)))
                def _():
                    ref[pl.ds(at, block_rows), :] = dk
                    ref[pl.ds(at + block_rows, block_rows), :] = dv

        return carry

    lax.fori_loop(first, last, flush, 0)
    if pad:
        gate = jnp.broadcast_to(jnp.sum(dots, axis=1, keepdims=True), (1, DH))
        own_ref[NY * n : NY * n + pad] = split_gate(gate)
        oth_ref[NY * n : NY * n + pad] = split_gate(gate)


def attention_grads(base, pad, max_blocks, ctx, bounds, low, high, gain, q, g, mine, others):
    tok = q.shape[0]
    merged = len(mine) == 1
    block_rows = mine[0].shape[-2]
    keys = NY * NZ * NCORE * block_rows
    pairs = GROUP * tok // PAIR
    steps = max_blocks * KB
    half = shaped((keys + pad, DH), BF16)
    return pl.pallas_call(
        functools.partial(attn_kernel, block_rows, base, pad, merged),
        out_shape=(shaped(q.shape, BF16), half, half),
        in_specs=[SMEM, SMEM] + [VMEM] * (5 + 2 * len(mine)),
        out_specs=(VMEM, VMEM, VMEM),
        scratch_shapes=[
            pltpu.VMEM((keys, DH), BF16),
            pltpu.VMEM((keys, DH), BF16),
            pltpu.VMEM((steps, PAIR), F32),
            pltpu.VMEM((steps, PAIR), F32),
            pltpu.VMEM((max_blocks, 1, PAIR), F32),
            pltpu.VMEM((max_blocks, DH, KB), BF16),
            pltpu.VMEM((pairs, DH, PAIR), BF16),
            pltpu.VMEM((pairs, DH, PAIR), BF16),
            pltpu.VMEM((pairs, PAIR, DH), BF16),
            pltpu.VMEM((pairs, PAIR, DH), BF16),
            pltpu.VMEM((steps, DH), F32),
            pltpu.VMEM((steps, DH), F32),
        ],
        cost_estimate=pl.CostEstimate(
            flops=10 * GROUP * tok * steps * DH,
            transcendentals=GROUP * tok * steps,
            bytes_accessed=2 * (3 * q.size + 4 * keys * DH),
        ),
        compiler_params=pltpu.CompilerParams(vmem_limit_bytes=32 * 1024 * 1024),
    )(ctx, bounds, low, high, gain, q, g, *mine, *others)


def local(
    query_self,
    key_self,
    value_self,
    grad_self,
    document_id,
    query_cross,
    image_keys,
    image_values,
    grad_cross,
    image_block,
    gate,
    w_key,
    w_value,
):
    tok = query_self.shape[0]
    img = image_keys.shape[0]
    seq = document_id.shape[0]
    ctx = lax.axis_index("ctx").reshape(1)
    tp = lax.axis_index("tp")

    kv, ikv = call(
        stack_kernel,
        (shaped((2, tok, DH), BF16), shaped((2, img, DH), BF16)),
        key_self,
        value_self,
        image_keys,
        image_values,
        params=None,
    )
    kv_z = [kv] + [send_z(kv, k) for k in range(1, NZ)]
    rows_doc = after(document_id.reshape(seq // tok, tok), kv)
    low, high, limit, gain, bounds = pl.pallas_call(
        rows_kernel,
        name="rows",
        out_shape=(shaped((1, PAIR), jnp.int32),) * 3
        + (shaped((8, DH), F32), shaped((8,), jnp.int32)),
        in_specs=[SMEM, SMEM, VMEM, VMEM],
        out_specs=(VMEM,) * 4 + (SMEM,),
        compiler_params=SMALL,
    )(ctx, gate, rows_doc, image_block.reshape(1, tok))
    pieces = weight_pieces(after(tp, bounds), w_key, w_value)
    kv_z[0] = after(kv_z[0], pieces[0])
    kv_mine = call(order_kernel, shaped((NZ, 2, tok, DH), BF16), ctx, *kv_z, smem=1)
    ikv = after(ikv, kv_mine)
    ikv_z = [ikv] + [send_z(ikv, k) for k in range(1, NZ)]
    mine = [kv_mine] + [send_y(kv_mine, k) for k in range(1, NY)]
    weights = [pieces[0]] + [send_x(pieces[k], k) for k in range(1, NX)]
    ikv_mine = call(order_kernel, shaped((NZ, 2, img, DH), BF16), ctx, *ikv_z, smem=1)
    others = [send_core(after(m, ikv_mine)) for m in mine]
    imine = [ikv_mine] + [send_y(ikv_mine, k) for k in range(1, NY)]
    query = after(query_self, ikv_mine)

    ones = jnp.ones((8, DH), F32)
    max_blocks = min((DOC_MAX - 1 + tok + KB - 2) // KB + 1, seq // KB)
    query_grad, own, other = attention_grads(
        0, 0, max_blocks, ctx, bounds, low, high, ones, query, grad_self, mine, others
    )
    got = send_core(other)
    imine = [after(m, own) for m in imine]
    iall = shaped((NY, NZ, 2, img, DH), BF16)
    imine = call(merge_kernel, iall, *imine)
    iothers = send_core(imine)
    piece = shaped((NZ * 2 * tok, DH), BF16)
    share = call(functools.partial(core_sum_kernel, 0), [piece] * NY, own, got)
    query = after(query_cross, share[0])
    share = [share[0]] + [send_y(share[k], k) for k in range(1, NY)]
    cross_query_grad, iown, iother = attention_grads(
        4,
        PAD,
        seq // 2 // KB,
        ctx,
        bounds,
        jnp.zeros((1, PAIR), jnp.int32),
        limit,
        gain,
        query,
        grad_cross,
        [imine],
        [iothers],
    )
    igot = send_core(iother)
    piece = shaped((2 * tok, DH), BF16)
    share[0] = after(share[0], iown)
    share = call(functools.partial(y_sum_kernel, 0), [piece] * NZ, ctx, *share, smem=1)
    iown = after(iown, share[0])
    share = [share[0]] + [send_z(share[k], k) for k in range(1, NZ)]
    ipiece = shaped((NZ * 2 * img + PAD, DH), BF16)
    ishare = call(functools.partial(core_sum_kernel, PAD), [ipiece] * NY, iown, igot)
    share[0] = after(share[0], ishare[0])
    ishare = [ishare[0]] + [send_y(ishare[k], k) for k in range(1, NY)]
    one = shaped((tok, DH), BF16)
    key_grad, value_grad, both = call(functools.partial(z_sum_kernel, 0), [one, one, piece], *share)
    ishare[0] = after(ishare[0], both)
    both = [both] + [send_x(both, k) for k in range(1, NX)]
    ipiece = shaped((2 * img + PAD, DH), BF16)
    ishare = call(functools.partial(y_sum_kernel, PAD), [ipiece] * NZ, ctx, *ishare, smem=1)
    both[0] = after(both[0], ishare[0])
    ishare = [ishare[0]] + [send_z(ishare[k], k) for k in range(1, NZ)]
    away = project(1, both, weights)
    both[0] = after(both[0], away)
    ishare[0] = after(ishare[0], away)
    away = send_zh(away)
    home = project(0, both, weights)
    ishare[0] = after(ishare[0], home)
    one = shaped((img, DH), BF16)
    gates = shaped((8, DH), F32)
    image_key_grad, image_value_grad, total = call(
        functools.partial(z_sum_kernel, PAD), [one, one, gates], *ishare
    )
    total = [total] + [send_x(total, k) for k in range(1, NX)]
    total = call(gate_sum_kernel, gates, *total)
    far = send_zh(total)
    gate_grad, input_grad = call(
        finish_kernel,
        [shaped((1, DH), F32), shaped(home.shape, BF16)],
        gain,
        total,
        far,
        home,
        away,
    )
    return (
        query_grad,
        key_grad,
        value_grad,
        input_grad,
        cross_query_grad,
        image_key_grad,
        image_value_grad,
        gate_grad[0, :1],
    )


def solution(mesh):
    two = P("ctx", "tp")
    in_specs = (two,) * 4 + (P(),) + (two,) * 4 + (P("ctx"), P(), P(None, "tp"), P(None, "tp"))
    out_specs = (two,) * 7 + (P(),)


    return jax.shard_map(local, mesh=mesh, in_specs=in_specs, out_specs=out_specs, check_vma=False)
```

```python
import functools
import math

import jax
import jax.numpy as jnp
from jax import lax
from jax.experimental import pallas as pl
from jax.experimental.pallas import tpu as pltpu
from jax.sharding import PartitionSpec as P


DH = 128
GROUP = 8
NIMG = 4
DOCS = 16
DOC_MAX = 2176

NEG_FILL = -1e30
MASKED = -2e30
SCALE = DH ** (-0.5)
LOG2E = math.log2(math.e)
KB = 256
PAIR = 1024
PAD = 16
NY, NZ, NCORE, NX = 4, 4, 2, 4

SMEM = pl.BlockSpec(memory_space=pltpu.SMEM)
VMEM = pl.BlockSpec(memory_space=pltpu.VMEM)
BF16 = jnp.bfloat16
F32 = jnp.float32

SMALL = pltpu.CompilerParams(vmem_limit_bytes=8 * 1024 * 1024)


def shaped(shape, dtype):
    return jax.ShapeDtypeStruct(shape, dtype)


def dot(a, b):
    return lax.dot_general(a, b, (((1,), (0,)), ((), ())), preferred_element_type=F32)


def dot_t(a, b):
    return lax.dot_general(a, b, (((1,), (1,)), ((), ())), preferred_element_type=F32)


def ctx_shift(dy, dz, flip):
    def move(c):
        y, z, core = c // 8, (c // 2) % 4, c % 2
        return ((y + dy) % NY) * 8 + ((z + dz) % NZ) * 2 + (core ^ flip)

    return [(c, move(c)) for c in range(NY * NZ * NCORE)]


def send_y(value, k):
    return lax.ppermute(value, "ctx", ctx_shift(k, 0, 0))


def send_z(value, k):
    return lax.ppermute(value, "ctx", ctx_shift(0, k, 0))


def send_core(value):
    return lax.ppermute(value, "ctx", ctx_shift(0, 0, 1))


def send_x(value, k, flip=0):
    perm = [(t, ((t // NX) ^ flip) * NX + (t + k) % NX) for t in range(2 * NX)]
    return lax.ppermute(value, "tp", perm)


def send_zh(value):
    return lax.ppermute(value, "tp", [(t, t ^ NX) for t in range(2 * NX)])


def after(value, *earlier):
    return lax.optimization_barrier((value,) + earlier)[0]


def stack_kernel(k_ref, v_ref, ik_ref, iv_ref, kv_ref, ikv_ref):
    kv_ref[0] = k_ref[...]
    kv_ref[1] = v_ref[...]
    ikv_ref[0] = ik_ref[...]
    ikv_ref[1] = iv_ref[...]


def rows_kernel(
    ctx_ref, gate_ref, doc_ref, block_ref, low_ref, high_ref, limit_ref, gain_ref, bounds_ref
):
    tok = doc_ref.shape[1]
    c = ctx_ref[0]
    docs = doc_ref[...]
    mine = doc_ref[pl.ds(c, 1), :]
    low = jnp.zeros((1, tok), jnp.int32)
    for d in range(1, DOCS):
        before = jnp.sum((docs < d).astype(F32), axis=0, keepdims=True)
        before = jnp.sum(before, axis=1, keepdims=True).astype(jnp.int32)
        low = jnp.where(mine == d, before, low)
    high = c * tok + lax.broadcasted_iota(jnp.int32, (1, tok), 1)
    limit = (block_ref[...] + 1) * (bounds_scale(doc_ref) // NIMG) - 1
    for i in range(PAIR // tok):
        low_ref[:, i * tok : (i + 1) * tok] = low
        high_ref[:, i * tok : (i + 1) * tok] = high
        limit_ref[:, i * tok : (i + 1) * tok] = limit
    gain_ref[...] = jnp.tanh(jnp.full(gain_ref.shape, gate_ref[0], F32))
    shift = KB.bit_length() - 1

    def put(at, first_key, clear_from, clear_to, last_key):
        first = lax.shift_right_logical(first_key, shift)
        last = lax.shift_right_logical(last_key, shift) + 1
        clear0 = lax.shift_right_logical(clear_from + KB - 1, shift)
        clear0 = jnp.minimum(jnp.maximum(clear0, first), last)
        clear1 = lax.shift_right_logical(clear_to + 1, shift)
        clear1 = jnp.minimum(jnp.maximum(clear1, clear0), last)
        for i, value in enumerate((first, clear0, clear1, last)):
            bounds_ref[at + i] = value

    put(0, jnp.min(low), jnp.max(low), c * tok, c * tok + tok - 1)
    put(4, jnp.int32(0), jnp.int32(0), jnp.min(limit), jnp.max(limit))


def bounds_scale(doc_ref):
    return doc_ref.shape[0] * doc_ref.shape[1] // 2


def order_kernel(ctx_ref, *refs):
    out_ref = refs[-1]
    z = lax.shift_right_logical(ctx_ref[0], 1) & (NZ - 1)
    for k in range(NZ):
        out_ref[(z - k) & (NZ - 1)] = refs[k][...]


def merge_kernel(*refs):
    for k in range(NY):
        refs[-1][k] = refs[k][...]


def weights_kernel(tp_ref, wk_ref, wv_ref, *refs):
    out_refs, held, came, left = refs[:NX], refs[NX], refs[NX + 1], refs[NX + 2]
    rows = held.shape[1]
    zh = lax.shift_right_logical(tp_ref[0], 2)
    x = tp_ref[0] & (NX - 1)
    ins, outs = [], []
    for k in (2, 1, 3, 0):
        for half in range(2):
            at = ((zh ^ half) * NX + ((x + k) & (NX - 1))) * rows
            at = pl.multiple_of(at, rows)
            for i, ref in enumerate((wk_ref, wv_ref)):
                n = len(ins)
                ins.append(
                    pltpu.make_async_copy(ref.at[pl.ds(at, rows), :], held.at[n], came.at[n])
                )
                outs.append(
                    pltpu.make_async_copy(held.at[n], out_refs[k].at[half, i], left.at[n])
                )
    for copy in ins:
        copy.start()
    for came_in, copy in zip(ins, outs):
        came_in.wait()
        copy.start()
    for copy in outs:
        copy.wait()


def weight_pieces(tp, w_key, w_value):
    rows = w_key.shape[0] // (2 * NX)
    whole = pl.BlockSpec(memory_space=pl.ANY)
    return pl.pallas_call(
        weights_kernel,
        name="weight_pieces",
        in_specs=[SMEM, whole, whole],
        out_specs=[whole] * NX,
        out_shape=[shaped((2, 2, rows, DH), BF16)] * NX,
        scratch_shapes=[
            pltpu.VMEM((4 * NX, rows, DH), BF16),
            pltpu.SemaphoreType.DMA((4 * NX,)),
            pltpu.SemaphoreType.DMA((4 * NX,)),
        ],
    )(tp, w_key, w_value)


def split_gate(total):
    hi = total.astype(BF16).astype(F32)
    mid = (total - hi).astype(BF16).astype(F32)
    lo = (total - hi) - mid
    row = lax.broadcasted_iota(jnp.int32, (PAD, DH), 0)
    rows = jnp.where(row == 0, hi, jnp.where(row == 1, mid, jnp.where(row == 2, lo, 0.0)))
    return rows.astype(BF16)


def join_gate(rows):
    return jnp.sum(rows.astype(F32), axis=0, keepdims=True)


def core_sum_kernel(pad, own_ref, other_ref, *out_refs):
    n = out_refs[0].shape[0] - pad
    if pad:
        at = NY * n
        tail = split_gate(join_gate(own_ref[at : at + pad]) + join_gate(other_ref[at : at + pad]))
    for k in range(NY):
        at = k * n
        total = own_ref[at : at + n].astype(F32) + other_ref[at : at + n].astype(F32)
        out_refs[k][0:n] = total.astype(BF16)
        if pad:
            out_refs[k][n : n + pad] = tail


def y_sum_kernel(pad, ctx_ref, s0_ref, s1_ref, s2_ref, s3_ref, *out_refs):
    n = out_refs[0].shape[0] - pad
    z = lax.shift_right_logical(ctx_ref[0], 1) & (NZ - 1)
    ins = (s0_ref, s1_ref, s2_ref, s3_ref)
    if pad:
        tail = split_gate(sum(join_gate(r[NZ * n : NZ * n + pad]) for r in ins))
    for k in range(NZ):
        at = pl.multiple_of(((z + k) & (NZ - 1)) * n, n)
        total = sum(r[pl.ds(at, n)].astype(F32) for r in ins)
        out_refs[k][0:n] = total.astype(BF16)
        if pad:
            out_refs[k][n : n + pad] = tail


def z_sum_kernel(gate_ref, s0_ref, s1_ref, s2_ref, s3_ref, k_ref, v_ref, both_ref):
    ins = (s0_ref, s1_ref, s2_ref, s3_ref)
    n = ins[0].shape[0]
    total = sum(r[...].astype(F32) for r in ins).astype(BF16)
    both_ref[0:n] = total
    both_ref[n : n + PAD] = gate_ref[...]
    k_ref[...] = total[: n // 2]
    v_ref[...] = total[n // 2 :]


def image_z_sum_kernel(s0_ref, s1_ref, s2_ref, s3_ref, k_ref, v_ref, gate_ref):
    ins = (s0_ref, s1_ref, s2_ref, s3_ref)
    n = ins[0].shape[0] - PAD
    total = sum(r[0:n].astype(F32) for r in ins).astype(BF16)
    gate_ref[...] = split_gate(sum(join_gate(r[n : n + PAD]) for r in ins))
    k_ref[...] = total[: n // 2]
    v_ref[...] = total[n // 2 :]


def project_kernel(half, *refs):
    grads, weights, out_ref = refs[:NX], refs[NX : 2 * NX], refs[2 * NX]
    tok = (grads[0].shape[0] - PAD) // 2
    cols = 256
    rows = weights[0].shape[2]
    if half:
        gate = split_gate(sum(join_gate(g[2 * tok : 2 * tok + PAD]) for g in grads))
        at = out_ref.shape[0] - PAD
        out_ref[at : at + PAD] = gate
    for j in range(rows // cols):
        total = None
        for g, w in zip(grads, weights):
            for i in range(2):
                part = dot_t(g[i * tok : (i + 1) * tok], w[half, i, j * cols : (j + 1) * cols])
                total = part if total is None else total + part
        if half:
            for i in range(cols // DH):
                at = (j * (cols // DH) + i) * tok
                out_ref[at : at + tok] = total[:, i * DH : (i + 1) * DH].astype(BF16)
        else:
            out_ref[:, j * cols : (j + 1) * cols] = total


def project(half, grads, weights):
    tok = (grads[0].shape[0] - PAD) // 2
    rows = weights[0].shape[2]
    return pl.pallas_call(
        functools.partial(project_kernel, half),
        in_specs=[VMEM] * (2 * NX),
        out_specs=VMEM,
        compiler_params=pltpu.CompilerParams(vmem_limit_bytes=16 * 1024 * 1024),
        out_shape=shaped((rows // DH * tok + PAD, DH), BF16) if half else shaped((tok, rows), F32),
        cost_estimate=pl.CostEstimate(
            flops=4 * NX * tok * rows * DH, transcendentals=0, bytes_accessed=4 * NX * rows * DH
        ),
    )(*grads, *weights)


def finish_kernel(gain_ref, near_ref, far_ref, home_ref, gate_ref, out_ref):
    tok, cols = home_ref.shape
    at = near_ref.shape[0] - PAD
    t = gain_ref[0:1, 0:DH]
    total = join_gate(near_ref[at : at + PAD]) + join_gate(far_ref[at : at + PAD])
    gate_ref[...] = (1.0 - t * t) * total
    for i in range(cols // DH):
        part = far_ref[i * tok : (i + 1) * tok].astype(F32)
        total = home_ref[:, i * DH : (i + 1) * DH] + part
        out_ref[:, i * DH : (i + 1) * DH] = total.astype(out_ref.dtype)


def call(kernel, outs, *args, smem=0, params=SMALL):
    single = not isinstance(outs, (list, tuple))
    specs = [SMEM] * smem + [VMEM] * (len(args) - smem)
    return pl.pallas_call(
        kernel,
        out_shape=outs,
        in_specs=specs,
        out_specs=VMEM if single else [VMEM] * len(outs),
        compiler_params=params,
    )(*args)


def attn_kernel(block_rows, base, pad, merged, *refs):
    ctx_ref, bounds_ref, low_ref, high_ref, gain_ref, q_ref, g_ref = refs[:7]
    if merged:
        mine, others = ([ref.at[k] for k in range(NY)] for ref in refs[7:9])
        refs = refs[9:]
    else:
        mine, others = refs[7 : 7 + NY], refs[7 + NY : 7 + 2 * NY]
        refs = refs[7 + 2 * NY :]
    dq_ref, own_ref, oth_ref = refs[:3]
    (k_s, v_s, e_s, d_s, peak_s, kt_s, qt_s, gt_s, qr_s, gr_s, dk_s, dv_s, dq_s) = refs[3:]
    first, clear0, clear1, last = (bounds_ref[base + i] for i in range(4))
    c = ctx_ref[0]
    core, my_y = c & 1, lax.shift_right_logical(c, 3)
    gain = gain_ref[0:1, 0:DH]
    low = low_ref[...]
    high = high_ref[...]
    tok = q_ref.shape[0]

    for h in range(GROUP):
        p, o = (h * tok) // PAIR, (h * tok) % PAIR
        qh = q_ref[:, h * DH : (h + 1) * DH]
        gh = g_ref[:, h * DH : (h + 1) * DH]
        qr_s[p, o : o + tok, :] = qh
        gr_s[p, o : o + tok, :] = gh
        qt_s[p, :, o : o + tok] = qh.T
        gt_s[p, :, o : o + tok] = gh.T
    for k in range(NY):
        for flip, ref in ((0, mine[k]), (1, others[k])):
            for z in range(NZ):
                block = ((my_y - k) & (NY - 1)) * 8 + z * 2 + (core ^ flip)
                at = pl.multiple_of(block * block_rows, block_rows)
                k_s[pl.ds(at, block_rows), :] = ref[z, 0]
                v_s[pl.ds(at, block_rows), :] = ref[z, 1]

    def prepare(b, carry):
        start = pl.multiple_of(b * KB, KB)
        kt_s[b - first] = k_s[pl.ds(start, KB), :].T
        where = pl.multiple_of((b - first) * KB, KB)
        dk_s[pl.ds(where, KB), :] = jnp.zeros((KB, DH), F32)
        dv_s[pl.ds(where, KB), :] = jnp.zeros((KB, DH), F32)
        return carry

    lax.fori_loop(first, last, prepare, 0)

    def one_pair(p, dot_total):
        qt = qt_s[p]
        gt = gt_s[p]

        def stats(masked, b, carry):
            peak, total, dsum = carry
            start = pl.multiple_of(b * KB, KB)
            where = pl.multiple_of((b - first) * KB, KB)
            s = dot(k_s[pl.ds(start, KB), :], qt)
            dp = dot(v_s[pl.ds(start, KB), :], gt)
            if masked:
                pos = lax.broadcasted_iota(jnp.int32, (KB, PAIR), 0)
                s = jnp.where((pos >= low - start) & (pos <= high - start), s, MASKED)
            new = jnp.maximum(peak, jnp.max(s, axis=0, keepdims=True))
            e = jnp.exp2((s - new) * (SCALE * LOG2E))
            factor = jnp.exp2((peak - new) * (SCALE * LOG2E))
            e_s[pl.ds(where, KB), :] = e
            d_s[pl.ds(where, KB), :] = dp
            peak_s[b - first] = new
            total = total * factor + jnp.sum(e, axis=0, keepdims=True)
            dsum = dsum * factor + jnp.sum(e * dp, axis=0, keepdims=True)
            return new, total, dsum

        carry = (
            jnp.full((1, PAIR), NEG_FILL, F32),
            jnp.zeros((1, PAIR), F32),
            jnp.zeros((1, PAIR), F32),
        )

        def edge(i, carry):
            b = first + i
            return stats(True, jnp.where(b < clear0, b, b + (clear1 - clear0)), carry)

        carry = lax.fori_loop(0, (last - first) - (clear1 - clear0), edge, carry)
        peak, total, dsum = lax.fori_loop(
            clear0, clear1, functools.partial(stats, False), carry
        )
        inv = 1.0 / total
        delta = dsum * inv

        def grads(b, carry):
            where = pl.multiple_of((b - first) * KB, KB)
            norm = jnp.exp2((peak_s[b - first] - peak) * (SCALE * LOG2E)) * inv
            prob = e_s[pl.ds(where, KB), :] * norm
            ds = (prob * (d_s[pl.ds(where, KB), :] - delta)).astype(BF16)
            dv_s[pl.ds(where, KB), :] += dot(prob.astype(BF16), gr_s[p])
            dk_s[pl.ds(where, KB), :] += dot(ds, qr_s[p])
            dq_s[...] += dot(kt_s[b - first], ds)
            return carry

        dq_s[...] = jnp.zeros((DH, PAIR), F32)
        lax.fori_loop(first, last, grads, 0)
        dqt = dq_s[...]
        for i in range(PAIR // tok):
            at = pl.multiple_of(p * (PAIR // tok) * DH + i * DH, DH)
            part = dqt[:, i * tok : (i + 1) * tok] * (gain * SCALE)
            dq_ref[:, pl.ds(at, DH)] = part.T.astype(BF16)
        return dot_total + delta

    dots = lax.fori_loop(0, GROUP * tok // PAIR, one_pair, jnp.zeros((1, PAIR), F32))

    n = NZ * 2 * block_rows
    per_step = KB // block_rows

    def flush(live, b, carry):
        for i in range(per_step):
            block = b * per_step + i
            k = (lax.shift_right_logical(block, 3) - my_y) & (NY - 1)
            z = lax.shift_right_logical(block, 1) & (NZ - 1)
            at = pl.multiple_of(k * n + z * 2 * block_rows, block_rows)
            if live:
                where = pl.multiple_of((b - first) * KB + i * block_rows, block_rows)
                dk = (dk_s[pl.ds(where, block_rows), :] * (gain * SCALE)).astype(BF16)
                dv = (dv_s[pl.ds(where, block_rows), :] * gain).astype(BF16)
            else:
                dk = dv = jnp.zeros((block_rows, DH), BF16)
            for same, ref in ((True, own_ref), (False, oth_ref)):

                @pl.when((core == (i & 1)) if same else (core != (i & 1)))
                def _():
                    ref[pl.ds(at, block_rows), :] = dk
                    ref[pl.ds(at + block_rows, block_rows), :] = dv

        return carry

    lax.fori_loop(0, first, functools.partial(flush, False), 0)
    lax.fori_loop(first, last, functools.partial(flush, True), 0)
    lax.fori_loop(last, k_s.shape[0] // KB, functools.partial(flush, False), 0)
    if pad:
        gate = jnp.broadcast_to(jnp.sum(dots, axis=1, keepdims=True), (1, DH))
        own_ref[NY * n : NY * n + pad] = split_gate(gate)
        oth_ref[NY * n : NY * n + pad] = split_gate(gate)


def attention_grads(base, pad, max_blocks, ctx, bounds, low, high, gain, q, g, mine, others):
    tok = q.shape[0]
    merged = len(mine) == 1
    block_rows = mine[0].shape[-2]
    keys = NY * NZ * NCORE * block_rows
    pairs = GROUP * tok // PAIR
    steps = max_blocks * KB
    half = shaped((keys + pad, DH), BF16)
    return pl.pallas_call(
        functools.partial(attn_kernel, block_rows, base, pad, merged),
        out_shape=(shaped(q.shape, BF16), half, half),
        in_specs=[SMEM, SMEM] + [VMEM] * (5 + 2 * len(mine)),
        out_specs=(VMEM, VMEM, VMEM),
        scratch_shapes=[
            pltpu.VMEM((keys, DH), BF16),
            pltpu.VMEM((keys, DH), BF16),
            pltpu.VMEM((steps, PAIR), F32),
            pltpu.VMEM((steps, PAIR), F32),
            pltpu.VMEM((max_blocks, 1, PAIR), F32),
            pltpu.VMEM((max_blocks, DH, KB), BF16),
            pltpu.VMEM((pairs, DH, PAIR), BF16),
            pltpu.VMEM((pairs, DH, PAIR), BF16),
            pltpu.VMEM((pairs, PAIR, DH), BF16),
            pltpu.VMEM((pairs, PAIR, DH), BF16),
            pltpu.VMEM((steps, DH), F32),
            pltpu.VMEM((steps, DH), F32),
            pltpu.VMEM((DH, PAIR), F32),
        ],
        cost_estimate=pl.CostEstimate(
            flops=10 * GROUP * tok * steps * DH,
            transcendentals=GROUP * tok * steps,
            bytes_accessed=2 * (3 * q.size + 4 * keys * DH),
        ),
        compiler_params=pltpu.CompilerParams(vmem_limit_bytes=32 * 1024 * 1024),
    )(ctx, bounds, low, high, gain, q, g, *mine, *others)


def local(
    query_self,
    key_self,
    value_self,
    grad_self,
    document_id,
    query_cross,
    image_keys,
    image_values,
    grad_cross,
    image_block,
    gate,
    w_key,
    w_value,
):
    tok = query_self.shape[0]
    img = image_keys.shape[0]
    seq = document_id.shape[0]
    ctx = lax.axis_index("ctx").reshape(1)
    tp = lax.axis_index("tp").reshape(1)

    kv, ikv = call(
        stack_kernel,
        (shaped((2, tok, DH), BF16), shaped((2, img, DH), BF16)),
        key_self,
        value_self,
        image_keys,
        image_values,
        params=None,
    )
    kv_z = [kv] + [send_z(kv, k) for k in range(1, NZ)]
    pieces = weight_pieces(after(tp, kv), w_key, w_value)
    kv_z[0] = after(kv_z[0], pieces[0])
    kv_mine = call(order_kernel, shaped((NZ, 2, tok, DH), BF16), ctx, *kv_z, smem=1)
    ikv = after(ikv, kv_mine)
    ikv_z = [ikv] + [send_z(ikv, k) for k in range(1, NZ)]
    mine = [kv_mine] + [send_y(kv_mine, k) for k in range(1, NY)]
    weights = [pieces[0]] + [send_x(pieces[k], k) for k in range(1, NX)]
    ikv_mine = call(order_kernel, shaped((NZ, 2, img, DH), BF16), ctx, *ikv_z, smem=1)
    others = [send_core(after(m, ikv_mine)) for m in mine]
    imine = [ikv_mine] + [send_y(ikv_mine, k) for k in range(1, NY)]
    rows_doc = after(document_id.reshape(seq // tok, tok), ikv_mine)
    low, high, limit, gain, bounds = pl.pallas_call(
        rows_kernel,
        name="rows",
        out_shape=(shaped((1, PAIR), jnp.int32),) * 3
        + (shaped((8, DH), F32), shaped((8,), jnp.int32)),
        in_specs=[SMEM, SMEM, VMEM, VMEM],
        out_specs=(VMEM,) * 4 + (SMEM,),
        compiler_params=SMALL,
    )(ctx, gate, rows_doc, image_block.reshape(1, tok))
    query = after(query_self, ikv_mine)

    ones = jnp.ones((8, DH), F32)
    max_blocks = min((DOC_MAX - 1 + tok + KB - 2) // KB + 1, seq // KB)
    query_grad, own, other = attention_grads(
        0, 0, max_blocks, ctx, bounds, low, high, ones, query, grad_self, mine, others
    )
    got = send_core(other)
    imine = [after(m, own) for m in imine]
    iall = shaped((NY, NZ, 2, img, DH), BF16)
    imine = call(merge_kernel, iall, *imine)
    iothers = send_core(imine)
    piece = shaped((NZ * 2 * tok, DH), BF16)
    share = call(functools.partial(core_sum_kernel, 0), [piece] * NY, own, got)
    query = after(query_cross, share[0])
    share = [share[0]] + [send_y(share[k], k) for k in range(1, NY)]
    cross_query_grad, iown, iother = attention_grads(
        4,
        PAD,
        seq // 2 // KB,
        ctx,
        bounds,
        jnp.zeros((1, PAIR), jnp.int32),
        limit,
        gain,
        query,
        grad_cross,
        [imine],
        [iothers],
    )
    igot = send_core(iother)
    ipiece = shaped((NZ * 2 * img + PAD, DH), BF16)
    ishare = call(functools.partial(core_sum_kernel, PAD), [ipiece] * NY, iown, igot)
    share[0] = after(share[0], ishare[0])
    ishare = [ishare[0]] + [send_y(ishare[k], k) for k in range(1, NY)]
    piece = shaped((2 * tok, DH), BF16)
    share = call(functools.partial(y_sum_kernel, 0), [piece] * NZ, ctx, *share, smem=1)
    ishare[0] = after(ishare[0], share[0])
    share = [share[0]] + [send_z(share[k], k) for k in range(1, NZ)]
    ipiece = shaped((2 * img + PAD, DH), BF16)
    ishare = call(functools.partial(y_sum_kernel, PAD), [ipiece] * NZ, ctx, *ishare, smem=1)
    ishare = [ishare[0]] + [send_z(ishare[k], k) for k in range(1, NZ)]
    one = shaped((img, DH), BF16)
    gates = shaped((PAD, DH), BF16)
    image_key_grad, image_value_grad, gates = call(image_z_sum_kernel, [one, one, gates], *ishare)
    one = shaped((tok, DH), BF16)
    both = shaped((2 * tok + PAD, DH), BF16)
    key_grad, value_grad, both = call(z_sum_kernel, [one, one, both], gates, *share)
    both = [both] + [send_x(both, k) for k in range(1, NX)]
    near = project(1, both, weights)
    both[0] = after(both[0], near)
    far = send_zh(near)
    home = project(0, both, weights)
    gate_grad, input_grad = call(
        finish_kernel, [shaped((1, DH), F32), shaped(home.shape, BF16)], gain, near, far, home
    )
    return (
        query_grad,
        key_grad,
        value_grad,
        input_grad,
        cross_query_grad,
        image_key_grad,
        image_value_grad,
        gate_grad[0, :1],
    )


def solution(mesh):
    two = P("ctx", "tp")
    in_specs = (two,) * 4 + (P(),) + (two,) * 4 + (P("ctx"), P(), P(None, "tp"), P(None, "tp"))
    out_specs = (two,) * 7 + (P(),)


    return jax.shard_map(local, mesh=mesh, in_specs=in_specs, out_specs=out_specs, check_vma=False)
```
